32 devices in a mesh: row: 4 (over y, x), col: 8 (over z, core).
Axes of the slice: x: 2, y: 2, z: 4, core: 2. Of those that a mesh axis runs over, the one named last changes fastest.
Arguments:
- intensity: float32 [16, 2048, 2048], P(None, 'row', 'col'), may hold values from -6 to 6
- punch_radius: int32 [2, 129, 129], replicated, may hold values from 0 to 12
Outputs:
- out_re: float32 [16, 2048, 2048], P(None, ('row', 'col'))
- out_im: float32 [16, 2048, 2048], P(None, ('row', 'col'))
The draws below stay inside these ranges and needn't reach their ends.
Inputs may be any that keep to these rules, and one draw needn't show every extreme that they name: `punch_radius`: squared radius in voxels; 0 leaves a node unpunched.
All inputs are finite; a program needn't handle non-finite values.
Results may differ from the reference program's by a relative error of at most 0.0029.
Values may be sent and summed in bfloat16 or wider, within the bound.
A program may use at most 128 MiB of HBM per device.

```python
import math
import jax
import jax.numpy as jnp
from jax import lax

N = 2048
SP = 16
L = 16
NODES = 128
LNODES = 2


def plant(array, own_key, smallest, largest):
    longest = array.shape.index(max(array.shape))
    spots = []
    for shift in (0, 1):
        where = [jax.random.randint(jax.random.fold_in(own_key, axis), (), 0, length) for axis, length in enumerate(array.shape)]
        where[longest] = (where[longest] + shift) % array.shape[longest]
        spots.append(tuple(where))
    return array.at[spots[0]].set(smallest).at[spots[1]].set(largest)


def block_scale(key, shape, cuts, least, high):
    gain = 1.0
    for position, parts in cuts:
        heights = jax.random.uniform(jax.random.fold_in(jax.random.fold_in(key, 6), position), (parts,), jnp.float32, least / len(cuts), high / len(cuts))
        gain = gain * jnp.repeat(jnp.exp(heights), shape[position] // parts).reshape((-1,) + (1,) * (len(shape) - 1 - position))
    return gain


def noise(key, extent, scale, reach, pieces=(), held_as=jnp.bfloat16):
    gain = block_scale(key, extent, pieces, -0.22, 0.18) if pieces else 1.0
    array = jax.random.normal(key, extent, jnp.float32) * scale * gain
    return jnp.minimum(jnp.maximum(array, -reach), reach).astype(held_as)


def setup_inputs(seed: int = 0) -> dict:
    splits = jax.random.split(jax.random.key(seed), 3)
    return {
        "intensity": noise(splits[0], (L, N, N), 1.0, 6.0, ((1, 4), (2, 8)), jnp.float32),
        "punch_radius": plant(jax.random.randint(splits[1], (LNODES, NODES + 1, NODES + 1), 0, 13), jax.random.fold_in(splits[1], 1), 0, 12).astype(jnp.int32),
    }


def circle(count, period, width):
    first_ids = jnp.arange(count, dtype=jnp.int32)
    second_ids = jnp.arange(width, dtype=jnp.int32)
    phases = (first_ids[:, None] * second_ids[None, :]) % period
    angles = phases.astype(jnp.float32) * (2.0 * math.pi / period)
    return jnp.cos(angles), jnp.sin(angles)


def mixed(form, left, right):
    return jnp.einsum(form, left, right, precision=lax.Precision.HIGHEST)


def spectral(real_in, imag_in):
    length = real_in.shape[-1]
    first = 32
    second = length // first
    shape_lead = real_in.shape[:-1]
    cos_first, sin_first = circle(first, first, first)
    cos_twist, sin_twist = circle(first, length, second)
    cos_second, sin_second = circle(second, second, second)
    grid_re = real_in.reshape(shape_lead + (first, second))
    section_re = mixed('...ab,ac->...cb', grid_re, cos_first)
    section_im = mixed('...ab,ac->...cb', grid_re, sin_first)
    if imag_in is not None:
        grid_im = imag_in.reshape(shape_lead + (first, second))
        section_re = section_re - mixed('...ab,ac->...cb', grid_im, sin_first)
        section_im = section_im + mixed('...ab,ac->...cb', grid_im, cos_first)
    twist_re = section_re * cos_twist - section_im * sin_twist
    twist_im = section_re * sin_twist + section_im * cos_twist
    final_re = mixed('...cb,bd->...dc', twist_re, cos_second) - mixed('...cb,bd->...dc', twist_im, sin_second)
    final_im = mixed('...cb,bd->...dc', twist_re, sin_second) + mixed('...cb,bd->...dc', twist_im, cos_second)
    return final_re.reshape(shape_lead + (length,)), final_im.reshape(shape_lead + (length,))


def reference(intensity, punch_radius):
    coords = jnp.arange(N, dtype=jnp.int32)
    node_of = (coords + SP // 2) // SP
    offsets = coords - SP * node_of
    dist_sq = offsets[:, None] * offsets[:, None] + offsets[None, :] * offsets[None, :]

    def plane(inputs):
        levels, values = inputs
        plane_node = (levels + SP // 2) // SP
        plane_off = levels - SP * plane_node
        radius_plane = punch_radius[plane_node]
        radius = radius_plane[node_of[:, None], node_of[None, :]]
        keep_mask = (dist_sq + plane_off * plane_off >= radius).astype(jnp.float32)
        keep_swap = keep_mask.T
        counts = jnp.maximum(keep_mask + keep_swap, 1.0)
        symmetric = ((keep_mask * values + keep_swap * values.T) / counts).astype(jnp.bfloat16)
        part_re, part_im = spectral(symmetric.astype(jnp.float32), None)
        real_out, imag_out = spectral(part_re.T, part_im.T)
        return real_out / N, imag_out / N

    plane_ids = jnp.arange(L, dtype=jnp.int32)
    out_re, out_im = lax.map(plane, (plane_ids, intensity))
    return out_re, out_im
```

```python
import math

import jax
import jax.numpy as jnp
from jax import lax
from jax.experimental import pallas as pl
from jax.experimental.pallas import tpu as pltpu
from jax.sharding import PartitionSpec as P

N = 2048
SP = 16


def circle(count, period, width):
    first_ids = jnp.arange(count, dtype=jnp.int32)
    second_ids = jnp.arange(width, dtype=jnp.int32)
    phases = first_ids[:, None] * second_ids[None, :] % period
    angles = phases.astype(jnp.float32) * (2.0 * math.pi / period)
    return (jnp.cos(angles), jnp.sin(angles))


def mixed(form, left, right):
    return jnp.einsum(form, left, right, precision=lax.Precision.HIGHEST)


def spectral(real_in, imag_in):
    length = real_in.shape[-1]
    first = 32
    second = length // first
    shape_lead = real_in.shape[:-1]
    cos_first, sin_first = circle(first, first, first)
    cos_twist, sin_twist = circle(first, length, second)
    cos_second, sin_second = circle(second, second, second)
    grid_re = real_in.reshape(shape_lead + (first, second))
    section_re = mixed("...ab,ac->...cb", grid_re, cos_first)
    section_im = mixed("...ab,ac->...cb", grid_re, sin_first)
    grid_im = imag_in.reshape(shape_lead + (first, second))
    section_re = section_re - mixed("...ab,ac->...cb", grid_im, sin_first)
    section_im = section_im + mixed("...ab,ac->...cb", grid_im, cos_first)
    twist_re = section_re * cos_twist - section_im * sin_twist
    twist_im = section_re * sin_twist + section_im * cos_twist
    final_re = mixed("...cb,bd->...dc", twist_re, cos_second) - mixed(
        "...cb,bd->...dc", twist_im, sin_second
    )
    final_im = mixed("...cb,bd->...dc", twist_re, sin_second) + mixed(
        "...cb,bd->...dc", twist_im, cos_second
    )
    return (final_re.reshape(shape_lead + (length,)), final_im.reshape(shape_lead + (length,)))


def spectral_lead(real_in):
    row_total, length = real_in.shape
    first = 32
    second = length // first
    cos_first, sin_first = circle(first, first, first)
    cos_twist, sin_twist = circle(first, length, second)
    cos_second, sin_second = circle(second, second, second)
    grid_re = real_in.reshape(row_total, first, second)
    section_re = mixed("rab,ac->cbr", grid_re, cos_first)
    section_im = mixed("rab,ac->cbr", grid_re, sin_first)
    twist_re = section_re * cos_twist[:, :, None] - section_im * sin_twist[:, :, None]
    twist_im = section_re * sin_twist[:, :, None] + section_im * cos_twist[:, :, None]
    final_re = mixed("cbr,bd->dcr", twist_re, cos_second) - mixed(
        "cbr,bd->dcr", twist_im, sin_second
    )
    final_im = mixed("cbr,bd->dcr", twist_re, sin_second) + mixed(
        "cbr,bd->dcr", twist_im, cos_second
    )
    return (final_re.reshape(length, row_total), final_im.reshape(length, row_total))


def keep_map(first_coords, second_coords, radius_table, levels):
    node_count = radius_table.shape[1]
    first_node = (first_coords + SP // 2) // SP
    first_dist = first_coords - SP * first_node
    second_node = (second_coords + SP // 2) // SP
    second_dist = second_coords - SP * second_node
    plane_node = (levels + SP // 2) // SP
    plane_dist = levels - SP * plane_node
    node_ids = jnp.arange(node_count, dtype=jnp.int32)
    pick_first = (first_node[:, None] == node_ids[None, :]).astype(jnp.bfloat16)
    pick_second = (second_node[:, None] == node_ids[None, :]).astype(jnp.bfloat16)
    table_half = jnp.einsum(
        "hn,snm->shm",
        pick_first,
        radius_table.astype(jnp.bfloat16),
        preferred_element_type=jnp.float32,
    ).astype(jnp.bfloat16)
    plane_radius = jnp.einsum(
        "shm,km->shk", table_half, pick_second, preferred_element_type=jnp.float32
    )
    level_ids = jnp.arange(radius_table.shape[0], dtype=jnp.int32)
    pick_plane = (plane_node[:, None] == level_ids[None, :]).astype(jnp.float32)
    radius = jnp.einsum("ls,shk->hlk", pick_plane, plane_radius, precision=lax.Precision.HIGHEST)
    distance = (
        (first_dist * first_dist)[:, None, None]
        + (plane_dist * plane_dist)[None, :, None]
        + (second_dist * second_dist)[None, None, :]
    )
    return (distance.astype(jnp.float32) >= radius).astype(jnp.float32)


def pencil_body(intensity, punch_radius):
    row_count = lax.axis_size("row")
    col_count = lax.axis_size("col")
    row_at = lax.axis_index("row")
    col_at = lax.axis_index("col")
    planes, h_block, k_block = intensity.shape
    groups = col_count // row_count
    fine_width = k_block // col_count
    pencil_rows = groups * fine_width
    levels = jnp.arange(planes, dtype=jnp.int32)
    swapped_table = jnp.swapaxes(punch_radius, 1, 2)
    outgoing = jnp.transpose(
        intensity.reshape(planes, h_block, col_count, fine_width), (2, 3, 0, 1)
    )
    arrived = lax.all_to_all(
        lax.all_to_all(outgoing, "col", split_axis=0, concat_axis=0, tiled=True),
        "row",
        split_axis=0,
        concat_axis=3,
        tiled=True,
    )
    pencil_h = (
        h_block * row_at
        + k_block * jnp.arange(groups, dtype=jnp.int32)[:, None]
        + fine_width * col_at
        + jnp.arange(fine_width, dtype=jnp.int32)[None, :]
    ).reshape(-1)
    whole_k = jnp.arange(N, dtype=jnp.int32)
    mirrored = arrived.reshape(pencil_rows, planes, N)
    pencil_input = jnp.transpose(
        intensity.reshape(planes, groups, col_count, fine_width, k_block), (1, 2, 3, 0, 4)
    )
    direct = lax.all_to_all(pencil_input, "col", split_axis=1, concat_axis=4, tiled=True).reshape(
        pencil_rows, planes, N
    )
    keep_mask = keep_map(pencil_h, whole_k, punch_radius, levels)
    keep_swap = keep_map(pencil_h, whole_k, swapped_table, levels)
    counts = jnp.maximum(keep_mask + keep_swap, 1.0)
    symmetric = ((keep_mask * direct + keep_swap * mirrored) / counts).astype(jnp.bfloat16)
    row_total = pencil_rows * planes
    flat_rows = symmetric.reshape(row_total, N).astype(jnp.float32)
    part_re, part_im = spectral_lead(flat_rows)
    freq_width = N // (row_count * col_count)
    sectioned = jnp.stack([part_re, part_im]).reshape(
        2, row_count, col_count, freq_width, row_total
    )
    spectra = lax.all_to_all(
        lax.all_to_all(sectioned, "row", split_axis=1, concat_axis=1, tiled=True),
        "col",
        split_axis=2,
        concat_axis=2,
        tiled=True,
    )
    spectra = spectra.reshape(2, row_count, col_count, freq_width, groups, fine_width, planes)
    spectra = jnp.transpose(spectra, (0, 6, 3, 1, 4, 2, 5)).reshape(2, planes * freq_width, N)
    final_re, final_im = spectral(spectra[0], spectra[1])
    out_re = (final_re / N).reshape(planes, freq_width, N)
    out_im = (final_im / N).reshape(planes, freq_width, N)
    return (out_re, out_im)


RADIX = 4
HALVES = 2
CORES = 2
CURVE = 7
CODE_BITS = 102
UNIT = 2.0**-CODE_BITS
LIMIT = 56 * 1024 * 1024


def spin(first_ids, second_ids, period):
    phases = first_ids * second_ids % period
    angles = phases.astype(jnp.float32) * (2.0 * math.pi / period)
    return jnp.cos(angles), jnp.sin(angles)


def halves(values):
    high = lax.reduce_precision(values, exponent_bits=8, mantissa_bits=7)
    return high.astype(jnp.bfloat16), (values - high).astype(jnp.bfloat16)


def packed(coarse, fine, shape):
    coarse_re, coarse_im = coarse
    fine_re, fine_im = fine
    full_re = (coarse_re * fine_re - coarse_im * fine_im).reshape(shape)
    full_im = (coarse_re * fine_im + coarse_im * fine_re).reshape(shape)
    return full_re, full_im


def dot32(left, right):
    return jnp.dot(left, right, preferred_element_type=jnp.float32)


def butterfly(res, ims):
    even_re, odd_re = res[0] + res[2], res[0] - res[2]
    even_im, odd_im = ims[0] + ims[2], ims[0] - ims[2]
    pair_re, gap_re = res[1] + res[3], res[1] - res[3]
    pair_im, gap_im = ims[1] + ims[3], ims[1] - ims[3]
    out_re = (even_re + pair_re, odd_re - gap_im, even_re - pair_re, odd_re + gap_im)
    out_im = (even_im + pair_im, odd_im + gap_re, even_im - pair_im, odd_im - gap_re)
    return out_re, out_im


def encode(values):
    size = jnp.exp2(jnp.log2(jnp.abs(values)) * (1.0 / CURVE)) * 2.0 ** (CODE_BITS / CURVE)
    return jnp.where(values < 0, -jnp.round(size), jnp.round(size)).astype(jnp.int16)


def decode(codes):
    base = codes.astype(jnp.float32)
    square = base * base
    return (square * square) * (square * base)


def mirror_kernel(tiles_ref, mirror_ref, send_sem, recv_sem):
    col = lax.axis_index("col")
    core = lax.rem(col, CORES)
    other = col + 1 - 2 * core
    barrier = pltpu.get_barrier_semaphore()
    pl.semaphore_signal(barrier, inc=1, device_id={"col": other})
    pl.semaphore_wait(barrier, 1)
    away = pltpu.make_async_remote_copy(
        src_ref=tiles_ref.at[:, :, 1 - core],
        dst_ref=mirror_ref,
        send_sem=send_sem,
        recv_sem=recv_sem,
        device_id={"col": other},
    )
    away.start()
    away.wait()


def mirror_tiles(tiles):
    rows, cols, _, size, _ = tiles.shape
    return pl.pallas_call(
        mirror_kernel,
        out_shape=jax.ShapeDtypeStruct((rows, cols, size, size), tiles.dtype),
        in_specs=[pl.BlockSpec(memory_space=pl.ANY)],
        out_specs=pl.BlockSpec(memory_space=pl.ANY),
        scratch_shapes=[pltpu.SemaphoreType.DMA] * 2,
        compiler_params=pltpu.CompilerParams(collective_id=0, has_side_effects=True),
        cost_estimate=pl.CostEstimate(
            flops=10**9, bytes_accessed=tiles.size * 2, transcendentals=0
        ),
    )(tiles)


def symmetrize(core_ref, direct_ref, own_ref, mirror_ref, near_ref, far_ref, pick_ref, order_ref, flip_ref, sym_ref):
    count, _, size, _ = direct_ref.shape
    width = 2 * size
    piece = width // RADIX
    rows = lax.broadcasted_iota(jnp.int32, (size, width), 0)
    cols = lax.broadcasted_iota(jnp.int32, (size, width), 1)
    row_off = (rows + SP // 2) % SP - SP // 2
    col_off = (cols + SP // 2) % SP - SP // 2
    distance = (row_off * row_off + col_off * col_off).astype(jnp.float32)
    pairs = count // 2
    here = pl.program_id(0) % CORES == core_ref[0]
    for pair in range(pairs):
        picked = pick_ref[:, pair * width : (pair + 1) * width]
        keep_mirror = distance >= dot32(near_ref[...], picked)
        keep_direct = distance >= dot32(far_ref[...], picked)
        turned = jnp.concatenate(
            [decode(direct_ref[2 * pair + at, 0].astype(jnp.int32)).T for at in range(2)], axis=1
        )
        across = jnp.concatenate(
            [
                decode(
                    jnp.where(
                        here,
                        own_ref[0, 2 * pair + at, 0].astype(jnp.int32),
                        mirror_ref[0, 2 * pair + at].astype(jnp.int32),
                    )
                )
                for at in range(2)
            ], axis=1
        )
        total = jnp.where(keep_mirror, across, 0.0) + jnp.where(keep_direct, turned, 0.0)
        scale = jnp.where(keep_mirror & keep_direct, 0.5 * UNIT, UNIT)
        sym = (total * scale).astype(jnp.bfloat16)
        sorted_rows = dot32(order_ref[...], sym).astype(jnp.bfloat16)
        ready = dot32(sorted_rows, flip_ref[...]).astype(jnp.bfloat16)
        ready = ready.reshape(RADIX, size // RADIX, width)
        for lead in range(RADIX):
            spot = (lead * pairs + pair) * piece
            sym_ref[:, :, spot : spot + piece] = ready[:, :, lead * piece : (lead + 1) * piece]


def transform_first(table_ref, sym_ref, part_ref):
    res, ims = [], []
    _, _, _, kinds, rows, width = table_ref.shape
    for lead in range(RADIX):
        data = sym_ref[lead]
        high = table_ref[0, lead, 0].reshape(kinds * rows, width)
        low = table_ref[1, lead, 0].reshape(kinds * rows, width)
        both = dot32(high, data) + dot32(low, data)
        res.append(both[:rows])
        ims.append(both[rows:])
    out_re, out_im = butterfly(res, ims)
    for block in range(RADIX):
        part_ref[0, block, 0] = out_re[block].astype(part_ref.dtype)
        part_ref[0, block, 1] = out_im[block].astype(part_ref.dtype)


def trade_kernel(part_ref, got_ref, send_sem, recv_sem):
    col = lax.axis_index("col")
    other = col + 1 - 2 * lax.rem(col, CORES)
    barrier = pltpu.get_barrier_semaphore()
    pl.semaphore_signal(barrier, inc=1, device_id={"col": other})
    pl.semaphore_wait(barrier, 1)
    copy = pltpu.make_async_remote_copy(
        src_ref=part_ref.at[1],
        dst_ref=got_ref,
        send_sem=send_sem,
        recv_sem=recv_sem,
        device_id={"col": other},
    )
    copy.start()
    copy.wait()


def trade(part):
    return pl.pallas_call(
        trade_kernel,
        out_shape=jax.ShapeDtypeStruct(part.shape[1:], part.dtype),
        in_specs=[pl.BlockSpec(memory_space=pl.ANY)],
        out_specs=pl.BlockSpec(memory_space=pl.ANY),
        scratch_shapes=[pltpu.SemaphoreType.DMA] * 2,
        compiler_params=pltpu.CompilerParams(collective_id=1, has_side_effects=True),
        cost_estimate=pl.CostEstimate(
            flops=10**9, bytes_accessed=part.size * 2, transcendentals=0
        ),
    )(part)


def second_kernel(scale, part_ref, other_ref, table_ref, got_ref, stage, send_sem, recv_sem, local_sem):
    row_count = lax.axis_size("row")
    row = lax.axis_index("row")
    col = lax.axis_index("col")
    core = lax.rem(col, CORES)
    _, deep, _, span, _ = stage.shape
    layer = lax.rem(col // CORES, deep)
    base = col - core - CORES * layer
    mine = row * deep + layer
    barrier = pltpu.get_barrier_semaphore()
    peers = [
        (lax.rem(row + step, row_count), lax.rem(layer + turn, deep))
        for step in range(row_count)
        for turn in range(deep)
        if step or turn
    ]
    for peer_row, peer_layer in peers:
        pl.semaphore_signal(
            barrier,
            inc=1,
            device_id={"row": peer_row, "col": base + CORES * peer_layer + core},
        )
    pl.semaphore_wait(barrier, len(peers))

    def out_copy(step, turn):
        to_row = lax.rem(row + step, row_count)
        to_layer = lax.rem(layer + turn, deep)
        return pltpu.make_async_remote_copy(
            src_ref=stage.at[to_row, to_layer],
            dst_ref=got_ref.at[mine],
            send_sem=send_sem.at[step * deep + turn],
            recv_sem=recv_sem.at[step * deep + turn],
            device_id={"row": to_row, "col": base + CORES * to_layer + core},
        )

    local = pltpu.make_async_copy(stage.at[row, layer], got_ref.at[mine], local_sem)
    half = part_ref.shape[-1] // RADIX
    for step in [*range(1, row_count), 0]:
        block = lax.rem(row + step, row_count)
        res, ims = [], []
        for lead in range(RADIX):
            data = jnp.concatenate(
                [
                    jnp.concatenate(
                        [
                            ref[0, block, kind, :, lead * half : (lead + 1) * half]
                            for ref in (part_ref, other_ref)
                        ],
                        axis=1,
                    )
                    for kind in range(2)
                ],
                axis=0,
            )
            rows = data.shape[0] // 2
            width = data.shape[1]
            both = dot32(data, table_ref[lead, :width]) + dot32(data, table_ref[lead, width:])
            res.append(both[:rows, :width] - both[rows:, width:])
            ims.append(both[:rows, width:] + both[rows:, :width])
        out_re, out_im = butterfly(res, ims)
        for kind, values in ((0, out_re), (1, out_im)):
            for part in range(RADIX):
                ready = (values[part] * scale).astype(stage.dtype)
                for at in range(deep):
                    stage[block, at, kind, :, part * width : (part + 1) * width] = ready[
                        at * span : (at + 1) * span
                    ]
        for turn in range(deep):
            if step or turn:
                out_copy(step, turn).start()
            else:
                local.start()
    local.wait()
    for step in range(row_count):
        for turn in range(deep):
            if step or turn:
                out_copy(step, turn).wait()


def second(part, other, table, scale, deep):
    _, blocks, _, rows, width = part.shape
    length = blocks * table.shape[-1] // 2
    span = rows // deep
    count = blocks * deep
    return pl.pallas_call(
        lambda *refs: second_kernel(scale, *refs),
        out_shape=jax.ShapeDtypeStruct((count, 2, span, length), part.dtype),
        grid=(1,),
        in_specs=[
            pl.BlockSpec((1, blocks, 2, rows, width), lambda at: (0, 0, 0, 0, 0)),
            pl.BlockSpec((1, blocks, 2, rows, width), lambda at: (0, 0, 0, 0, 0)),
            pl.BlockSpec(table.shape, lambda at: (0, 0, 0)),
        ],
        out_specs=pl.BlockSpec(memory_space=pl.ANY),
        scratch_shapes=[
            pltpu.VMEM((blocks, deep, 2, span, length), part.dtype),
            pltpu.SemaphoreType.DMA((count,)),
            pltpu.SemaphoreType.DMA((count,)),
            pltpu.SemaphoreType.DMA,
        ],
        compiler_params=pltpu.CompilerParams(
            collective_id=2, has_side_effects=True, vmem_limit_bytes=LIMIT
        ),
        cost_estimate=pl.CostEstimate(
            flops=50 * 10**9, bytes_accessed=10**7, transcendentals=0
        ),
    )(part, other[None], table)


def widen_kernel(got_ref, *refs):
    re_ref, im_ref = refs[-2:]
    re_ref[...] = got_ref[:, 0].astype(jnp.float32)
    im_ref[...] = got_ref[:, 1].astype(jnp.float32)


def widen(at, rounds, received, outs):
    count, _, rows, length = received.shape
    lot = 2
    shape = jax.ShapeDtypeStruct((rounds * count, rows, length), jnp.float32)
    spec = pl.BlockSpec((lot, rows, length), lambda c: (at * (count // lot) + c, 0, 0))
    return pl.pallas_call(
        widen_kernel,
        out_shape=(shape, shape),
        grid=(count // lot,),
        in_specs=[pl.BlockSpec((lot, 2, rows, length), lambda c: (c, 0, 0, 0))]
        + [pl.BlockSpec(memory_space=pl.ANY)] * len(outs),
        out_specs=(spec, spec),
        input_output_aliases={1 + which: which for which in range(len(outs))},
        compiler_params=pltpu.CompilerParams(vmem_limit_bytes=LIMIT),
        cost_estimate=pl.CostEstimate(
            flops=8 * 10**9, bytes_accessed=received.size * 6, transcendentals=0
        ),
    )(received, *outs)


def plane_body(intensity, punch_radius):
    row_count = lax.axis_size("row")
    col_count = lax.axis_size("col")
    row = lax.axis_index("row")
    col = lax.axis_index("col")
    core = col % CORES
    deep = col_count // (HALVES * CORES)
    layer = col // CORES % deep
    half = col // (CORES * deep)
    planes, h_block, size = intensity.shape
    length = h_block * row_count
    width = length // RADIX
    lot = row_count * deep
    rounds = planes // lot
    span = length // (row_count * col_count)
    bf16 = jnp.bfloat16

    node_count = punch_radius.shape[1]
    node_ids = jnp.arange(node_count, dtype=jnp.int32)
    whole = jnp.arange(length, dtype=jnp.int32)
    inner = jnp.arange(size, dtype=jnp.int32)
    tile_rows = jnp.arange(row_count, dtype=jnp.int32)
    pick_k = ((whole[:, None] + SP // 2) // SP == node_ids[None, :]).astype(bf16)
    mine = ((CORES * tile_rows + core)[:, None] * size + inner[None, :]).reshape(-1)
    pick_h = ((mine[None, :] + SP // 2) // SP == node_ids[:, None]).astype(bf16)

    def limits(at):
        level = at * lot + row * deep + layer
        node = (level + SP // 2) // SP
        off = level - SP * node
        table = lax.dynamic_index_in_dim(punch_radius, node, 0, keepdims=False) - off * off
        table = table.astype(bf16)
        near = jnp.einsum("kn,nm->km", pick_k, table, preferred_element_type=jnp.float32)
        far = jnp.einsum("kn,mn->km", pick_k, table, preferred_element_type=jnp.float32)
        return near.astype(bf16), far.astype(bf16)

    local = jnp.arange(size, dtype=jnp.int32)
    source = RADIX * (local % (size // RADIX)) + local // (size // RADIX)
    order = (source[:, None] == local[None, :]).astype(bf16)
    wide = jnp.arange(2 * size, dtype=jnp.int32)
    lead_of = wide // (2 * size // RADIX)
    tile_of = wide // (size // RADIX) % 2
    from_wide = tile_of * size + RADIX * (wide % (size // RADIX)) + lead_of
    flip = (from_wide[None, :] == wide[:, None]).astype(bf16)

    fine = 16
    lead_ids = jnp.arange(RADIX, dtype=jnp.int32)
    low_ids = jnp.arange(fine, dtype=jnp.int32)
    minor = jnp.arange(width, dtype=jnp.int32)
    sides = jnp.stack([core, 1 - core])
    layers = jnp.arange(deep, dtype=jnp.int32)
    starts = (
        half * (width // HALVES)
        + CORES * span * layers[None, :, None]
        + span * sides[:, None, None]
        + fine * jnp.arange(span // fine, dtype=jnp.int32)[None, None, :]
    ).reshape(-1)
    sample = RADIX * minor[None, None, None, :] + lead_ids[:, None, None, None]
    freq = packed(
        spin(sample, starts[None, :, None, None], length),
        spin(sample, low_ids[None, None, :, None], length),
        (RADIX, CORES, 1, deep * span, width),
    )
    freq_table = jnp.stack(halves(jnp.concatenate(freq, axis=2)))
    piece = size // RADIX
    blocks = (
        piece * (CORES * tile_rows[None, :, None] + sides[:, None, None])
        + fine * jnp.arange(piece // fine, dtype=jnp.int32)[None, None, :]
    ).reshape(-1)
    time = packed(
        spin(RADIX * blocks[None, :, None, None], minor, length),
        spin(RADIX * low_ids[None, None, :, None] + lead_ids[:, None, None, None], minor, length),
        (RADIX, width, width),
    )
    time_table = jnp.concatenate(halves(jnp.concatenate(time, axis=2)), axis=1)

    params = pltpu.CompilerParams(vmem_limit_bytes=LIMIT)
    order_like = (row_count, 1, deep, CORES, size, size)

    def gather(at):
        block = intensity[at * lot : (at + 1) * lot]
        coded = encode(block).reshape(order_like)
        spread = jnp.broadcast_to(coded, (row_count, HALVES) + order_like[2:])
        return lax.all_to_all(
            spread.reshape(-1, size, size), ("row", "col"), split_axis=0, concat_axis=0, tiled=True
        )

    def blend(tiles, mirrored, near, far):
        spot = jnp.full((1,), core, jnp.int32)
        return pl.pallas_call(
            symmetrize,
            out_shape=jax.ShapeDtypeStruct((RADIX, width, row_count * size), bf16),
            grid_spec=pltpu.PrefetchScalarGridSpec(
                num_scalar_prefetch=1,
                grid=(col_count,),
                in_specs=[
                    pl.BlockSpec((row_count, 1, size, size), lambda j, c: (0, j, 0, 0)),
                    pl.BlockSpec(
                        (1, row_count, 1, size, size), lambda j, c: (j // 2, 0, c[0], 0, 0)
                    ),
                    pl.BlockSpec((1, row_count, size, size), lambda j, c: (j // 2, 0, 0, 0)),
                    pl.BlockSpec((size, node_count), lambda j, c: (j, 0)),
                    pl.BlockSpec((size, node_count), lambda j, c: (j, 0)),
                    pl.BlockSpec((node_count, row_count * size), lambda j, c: (0, 0)),
                    pl.BlockSpec((size, size), lambda j, c: (0, 0)),
                    pl.BlockSpec((2 * size, 2 * size), lambda j, c: (0, 0)),
                ],
                out_specs=pl.BlockSpec(
                    (RADIX, size // RADIX, row_count * size), lambda j, c: (0, j, 0)
                ),
            ),
            compiler_params=params,
            cost_estimate=pl.CostEstimate(
                flops=14 * 10**9, bytes_accessed=10**7, transcendentals=0
            ),
        )(
            spot,
            tiles.reshape(row_count, col_count, size, size),
            tiles.reshape(row_count, row_count, CORES, size, size),
            mirrored,
            near,
            far,
            pick_h,
            order,
            flip,
        )

    def first(sym):
        rows = deep * span
        return pl.pallas_call(
            transform_first,
            out_shape=jax.ShapeDtypeStruct((CORES, RADIX, 2, rows, row_count * size), bf16),
            grid=(CORES,),
            in_specs=[
                pl.BlockSpec((2, RADIX, 1, 2, rows, width), lambda d: (0, 0, d, 0, 0, 0)),
                pl.BlockSpec((RADIX, width, row_count * size), lambda d: (0, 0, 0)),
            ],
            out_specs=pl.BlockSpec(
                (1, RADIX, 2, rows, row_count * size), lambda d: (d, 0, 0, 0, 0)
            ),
            compiler_params=params,
            cost_estimate=pl.CostEstimate(
                flops=14 * 10**9, bytes_accessed=10**7, transcendentals=0
            ),
        )(freq_table.reshape(2, RADIX, CORES, 2, rows, width), sym)

    outs = ()
    coming = gather(0)
    for at in range(rounds):
        tiles = coming
        if at + 1 < rounds:
            coming = gather(at + 1)
        near, far = limits(at)
        mirrored = mirror_tiles(tiles.reshape(row_count, row_count, CORES, size, size))
        sym = blend(tiles, mirrored, near, far)
        part = first(sym)
        received = second(part, trade(part), time_table, 1.0 / length, deep)
        if at + 1 < rounds:
            received, coming = lax.optimization_barrier((received, coming))
        outs = widen(at, rounds, received, outs)
    return outs


def body(intensity, punch_radius):
    row_count = lax.axis_size("row")
    col_count = lax.axis_size("col")
    planes, _, k_block = intensity.shape
    by_plane = row_count == RADIX and col_count == HALVES * RADIX
    by_plane = by_plane and planes % (row_count * col_count // RADIX) == 0 and k_block % 256 == 0
    return (plane_body if by_plane else pencil_body)(intensity, punch_radius)


def solution(mesh):
    in_specs = (P(None, "row", "col"), P())
    out_specs = (P(None, ("row", "col"), None), P(None, ("row", "col"), None))
    return jax.shard_map(body, mesh=mesh, in_specs=in_specs, out_specs=out_specs, check_vma=False)
```

```python
import math

import jax
import jax.numpy as jnp
from jax import lax
from jax.experimental import pallas as pl
from jax.experimental.pallas import tpu as pltpu
from jax.sharding import PartitionSpec as P

N = 2048
SP = 16


def circle(count, period, width):
    first_ids = jnp.arange(count, dtype=jnp.int32)
    second_ids = jnp.arange(width, dtype=jnp.int32)
    phases = first_ids[:, None] * second_ids[None, :] % period
    angles = phases.astype(jnp.float32) * (2.0 * math.pi / period)
    return (jnp.cos(angles), jnp.sin(angles))


def mixed(form, left, right):
    return jnp.einsum(form, left, right, precision=lax.Precision.HIGHEST)


def spectral(real_in, imag_in):
    length = real_in.shape[-1]
    first = 32
    second = length // first
    shape_lead = real_in.shape[:-1]
    cos_first, sin_first = circle(first, first, first)
    cos_twist, sin_twist = circle(first, length, second)
    cos_second, sin_second = circle(second, second, second)
    grid_re = real_in.reshape(shape_lead + (first, second))
    section_re = mixed("...ab,ac->...cb", grid_re, cos_first)
    section_im = mixed("...ab,ac->...cb", grid_re, sin_first)
    grid_im = imag_in.reshape(shape_lead + (first, second))
    section_re = section_re - mixed("...ab,ac->...cb", grid_im, sin_first)
    section_im = section_im + mixed("...ab,ac->...cb", grid_im, cos_first)
    twist_re = section_re * cos_twist - section_im * sin_twist
    twist_im = section_re * sin_twist + section_im * cos_twist
    final_re = mixed("...cb,bd->...dc", twist_re, cos_second) - mixed(
        "...cb,bd->...dc", twist_im, sin_second
    )
    final_im = mixed("...cb,bd->...dc", twist_re, sin_second) + mixed(
        "...cb,bd->...dc", twist_im, cos_second
    )
    return (final_re.reshape(shape_lead + (length,)), final_im.reshape(shape_lead + (length,)))


def spectral_lead(real_in):
    row_total, length = real_in.shape
    first = 32
    second = length // first
    cos_first, sin_first = circle(first, first, first)
    cos_twist, sin_twist = circle(first, length, second)
    cos_second, sin_second = circle(second, second, second)
    grid_re = real_in.reshape(row_total, first, second)
    section_re = mixed("rab,ac->cbr", grid_re, cos_first)
    section_im = mixed("rab,ac->cbr", grid_re, sin_first)
    twist_re = section_re * cos_twist[:, :, None] - section_im * sin_twist[:, :, None]
    twist_im = section_re * sin_twist[:, :, None] + section_im * cos_twist[:, :, None]
    final_re = mixed("cbr,bd->dcr", twist_re, cos_second) - mixed(
        "cbr,bd->dcr", twist_im, sin_second
    )
    final_im = mixed("cbr,bd->dcr", twist_re, sin_second) + mixed(
        "cbr,bd->dcr", twist_im, cos_second
    )
    return (final_re.reshape(length, row_total), final_im.reshape(length, row_total))


def keep_map(first_coords, second_coords, radius_table, levels):
    node_count = radius_table.shape[1]
    first_node = (first_coords + SP // 2) // SP
    first_dist = first_coords - SP * first_node
    second_node = (second_coords + SP // 2) // SP
    second_dist = second_coords - SP * second_node
    plane_node = (levels + SP // 2) // SP
    plane_dist = levels - SP * plane_node
    node_ids = jnp.arange(node_count, dtype=jnp.int32)
    pick_first = (first_node[:, None] == node_ids[None, :]).astype(jnp.bfloat16)
    pick_second = (second_node[:, None] == node_ids[None, :]).astype(jnp.bfloat16)
    table_half = jnp.einsum(
        "hn,snm->shm",
        pick_first,
        radius_table.astype(jnp.bfloat16),
        preferred_element_type=jnp.float32,
    ).astype(jnp.bfloat16)
    plane_radius = jnp.einsum(
        "shm,km->shk", table_half, pick_second, preferred_element_type=jnp.float32
    )
    level_ids = jnp.arange(radius_table.shape[0], dtype=jnp.int32)
    pick_plane = (plane_node[:, None] == level_ids[None, :]).astype(jnp.float32)
    radius = jnp.einsum("ls,shk->hlk", pick_plane, plane_radius, precision=lax.Precision.HIGHEST)
    distance = (
        (first_dist * first_dist)[:, None, None]
        + (plane_dist * plane_dist)[None, :, None]
        + (second_dist * second_dist)[None, None, :]
    )
    return (distance.astype(jnp.float32) >= radius).astype(jnp.float32)


def pencil_body(intensity, punch_radius):
    row_count = lax.axis_size("row")
    col_count = lax.axis_size("col")
    row_at = lax.axis_index("row")
    col_at = lax.axis_index("col")
    planes, h_block, k_block = intensity.shape
    groups = col_count // row_count
    fine_width = k_block // col_count
    pencil_rows = groups * fine_width
    levels = jnp.arange(planes, dtype=jnp.int32)
    swapped_table = jnp.swapaxes(punch_radius, 1, 2)
    outgoing = jnp.transpose(
        intensity.reshape(planes, h_block, col_count, fine_width), (2, 3, 0, 1)
    )
    arrived = lax.all_to_all(
        lax.all_to_all(outgoing, "col", split_axis=0, concat_axis=0, tiled=True),
        "row",
        split_axis=0,
        concat_axis=3,
        tiled=True,
    )
    pencil_h = (
        h_block * row_at
        + k_block * jnp.arange(groups, dtype=jnp.int32)[:, None]
        + fine_width * col_at
        + jnp.arange(fine_width, dtype=jnp.int32)[None, :]
    ).reshape(-1)
    whole_k = jnp.arange(N, dtype=jnp.int32)
    mirrored = arrived.reshape(pencil_rows, planes, N)
    pencil_input = jnp.transpose(
        intensity.reshape(planes, groups, col_count, fine_width, k_block), (1, 2, 3, 0, 4)
    )
    direct = lax.all_to_all(pencil_input, "col", split_axis=1, concat_axis=4, tiled=True).reshape(
        pencil_rows, planes, N
    )
    keep_mask = keep_map(pencil_h, whole_k, punch_radius, levels)
    keep_swap = keep_map(pencil_h, whole_k, swapped_table, levels)
    counts = jnp.maximum(keep_mask + keep_swap, 1.0)
    symmetric = ((keep_mask * direct + keep_swap * mirrored) / counts).astype(jnp.bfloat16)
    row_total = pencil_rows * planes
    flat_rows = symmetric.reshape(row_total, N).astype(jnp.float32)
    part_re, part_im = spectral_lead(flat_rows)
    freq_width = N // (row_count * col_count)
    sectioned = jnp.stack([part_re, part_im]).reshape(
        2, row_count, col_count, freq_width, row_total
    )
    spectra = lax.all_to_all(
        lax.all_to_all(sectioned, "row", split_axis=1, concat_axis=1, tiled=True),
        "col",
        split_axis=2,
        concat_axis=2,
        tiled=True,
    )
    spectra = spectra.reshape(2, row_count, col_count, freq_width, groups, fine_width, planes)
    spectra = jnp.transpose(spectra, (0, 6, 3, 1, 4, 2, 5)).reshape(2, planes * freq_width, N)
    final_re, final_im = spectral(spectra[0], spectra[1])
    out_re = (final_re / N).reshape(planes, freq_width, N)
    out_im = (final_im / N).reshape(planes, freq_width, N)
    return (out_re, out_im)


RADIX = 4
HALVES = 2
CORES = 2
CURVE = 7
CODE_BITS = 102
UNIT = 2.0**-CODE_BITS
LIMIT = 56 * 1024 * 1024


def spin(first_ids, second_ids, period):
    phases = first_ids * second_ids % period
    angles = phases.astype(jnp.float32) * (2.0 * math.pi / period)
    return jnp.cos(angles), jnp.sin(angles)


def halves(values):
    high = lax.reduce_precision(values, exponent_bits=8, mantissa_bits=7)
    return high.astype(jnp.bfloat16), (values - high).astype(jnp.bfloat16)


def packed(coarse, fine, shape):
    coarse_re, coarse_im = coarse
    fine_re, fine_im = fine
    full_re = (coarse_re * fine_re - coarse_im * fine_im).reshape(shape)
    full_im = (coarse_re * fine_im + coarse_im * fine_re).reshape(shape)
    return full_re, full_im


def dot32(left, right):
    return jnp.dot(left, right, preferred_element_type=jnp.float32)


def butterfly(res, ims):
    even_re, odd_re = res[0] + res[2], res[0] - res[2]
    even_im, odd_im = ims[0] + ims[2], ims[0] - ims[2]
    pair_re, gap_re = res[1] + res[3], res[1] - res[3]
    pair_im, gap_im = ims[1] + ims[3], ims[1] - ims[3]
    out_re = (even_re + pair_re, odd_re - gap_im, even_re - pair_re, odd_re + gap_im)
    out_im = (even_im + pair_im, odd_im + gap_re, even_im - pair_im, odd_im - gap_re)
    return out_re, out_im


def encode(values):
    size = jnp.exp2(jnp.log2(jnp.abs(values)) * (1.0 / CURVE)) * 2.0 ** (CODE_BITS / CURVE)
    return jnp.where(values < 0, -jnp.round(size), jnp.round(size)).astype(jnp.int16)


def decode(codes):
    base = codes.astype(jnp.int32).astype(jnp.float32)
    square = base * base
    return (square * square) * (square * base)


def keep_scale(near, far, picked, distance):
    keep_mirror = distance >= dot32(near, picked)
    keep_direct = distance >= dot32(far, picked)
    scale = jnp.where(keep_mirror & keep_direct, 0.5 * UNIT, UNIT)
    return jnp.where(keep_mirror, scale, 0.0), jnp.where(keep_direct, scale, 0.0)


def plane_kernel(
    scale,
    tiles_ref,
    near_ref,
    far_ref,
    pick_ref,
    order_ref,
    flip_ref,
    freq_hbm,
    time_hbm,
    got_ref,
    tiles,
    mirror,
    sym,
    freq,
    time,
    part,
    other,
    stage,
    load_sem,
    swap_sem,
    send_sem,
    recv_sem,
):
    row_count = lax.axis_size("row")
    row = lax.axis_index("row")
    col = lax.axis_index("col")
    core = lax.rem(col, CORES)
    deep, span = stage.shape[1], stage.shape[3]
    size = tiles.shape[-1]
    layer = lax.rem(col // CORES, deep)
    base = col - core - CORES * layer
    mine = row * deep + layer
    twin = {"col": col + 1 - 2 * core}

    loads = [
        pltpu.make_async_copy(tiles_ref, tiles, load_sem.at[0]),
        pltpu.make_async_copy(freq_hbm, freq, load_sem.at[1]),
        pltpu.make_async_copy(time_hbm, time, load_sem.at[2]),
    ]
    for load in loads:
        load.start()

    barrier = pltpu.get_barrier_semaphore()
    turns = [(step, turn) for step in range(row_count) for turn in range(deep) if step or turn]

    def place(step, turn):
        return {
            "row": lax.rem(row + step, row_count),
            "col": base + CORES * lax.rem(layer + turn, deep) + core,
        }

    pl.semaphore_signal(barrier, inc=1, device_id=twin)
    for step, turn in turns:
        pl.semaphore_signal(barrier, inc=1, device_id=place(step, turn))
    pl.semaphore_wait(barrier, 1 + len(turns))

    away = pltpu.make_async_remote_copy(
        src_ref=tiles_ref.at[:, :, 1 - core],
        dst_ref=mirror,
        send_sem=swap_sem.at[0],
        recv_sem=swap_sem.at[1],
        device_id=twin,
    )
    away.start()

    width = 2 * size
    piece = width // RADIX
    pairs = row_count // 2
    rows = lax.broadcasted_iota(jnp.int32, (size, width), 0)
    cols = lax.broadcasted_iota(jnp.int32, (size, width), 1)
    row_off = (rows + SP // 2) % SP - SP // 2
    col_off = (cols + SP // 2) % SP - SP // 2
    distance = (row_off * row_off + col_off * col_off).astype(jnp.float32)

    def blend(block, parity, reflected):
        at = pl.multiple_of((CORES * block + parity) * size, size)
        for pair in range(pairs):
            picked = pick_ref[:, pair * width : (pair + 1) * width]
            by_mirror, by_direct = keep_scale(
                near_ref[pl.ds(at, size)], far_ref[pl.ds(at, size)], picked, distance
            )
            turned = jnp.concatenate(
                [decode(tiles[2 * pair + up, block, parity]).T for up in range(2)], axis=1
            )
            across = jnp.concatenate(
                [decode(reflected(block, 2 * pair + up)) for up in range(2)], axis=1
            )
            total = by_mirror * across + by_direct * turned
            half = dot32(order_ref[...], total.astype(jnp.bfloat16)).astype(jnp.bfloat16)
            ready = dot32(half, flip_ref[...]).astype(jnp.bfloat16)
            ready = ready.reshape(RADIX, size // RADIX, width)
            spot = pl.multiple_of((CORES * block + parity) * (size // RADIX), size // RADIX)
            for lead in range(RADIX):
                start = (lead * pairs + pair) * piece
                sym[:, pl.ds(spot, size // RADIX), start : start + piece] = ready[
                    :, :, lead * piece : (lead + 1) * piece
                ]

    loads[0].wait()

    @pl.loop(0, row_count)
    def _(block):
        blend(block, core, lambda at, up: tiles[at, up, core])

    away.wait()

    @pl.loop(0, row_count)
    def _(block):
        blend(block, 1 - core, lambda at, up: mirror[at, up])

    loads[1].wait()
    trade = pltpu.make_async_remote_copy(
        src_ref=part.at[1],
        dst_ref=other,
        send_sem=swap_sem.at[2],
        recv_sem=swap_sem.at[3],
        device_id=twin,
    )
    count = part.shape[3]
    for side in (1, 0):
        res, ims = [], []
        for lead in range(RADIX):
            data = sym[lead]
            high = freq[0, lead, side].reshape(2 * count, -1)
            low = freq[1, lead, side].reshape(2 * count, -1)
            both = dot32(high, data) + dot32(low, data)
            res.append(both[:count])
            ims.append(both[count:])
        out_re, out_im = butterfly(res, ims)
        for block in range(RADIX):
            part[side, block, 0] = out_re[block].astype(part.dtype)
            part[side, block, 1] = out_im[block].astype(part.dtype)
        if side:
            trade.start()

    loads[2].wait()
    trade.wait()

    def out_copy(step, turn):
        to_row = lax.rem(row + step, row_count)
        to_layer = lax.rem(layer + turn, deep)
        return pltpu.make_async_remote_copy(
            src_ref=stage.at[to_row, to_layer],
            dst_ref=got_ref.at[mine],
            send_sem=send_sem.at[step * deep + turn],
            recv_sem=recv_sem.at[step * deep + turn],
            device_id=place(step, turn),
        )

    local = pltpu.make_async_copy(stage.at[row, layer], got_ref.at[mine], load_sem.at[3])
    half = part.shape[-1] // RADIX

    @pl.loop(0, row_count)
    def _(tick):
        step = lax.rem(tick + 1, row_count)
        block = lax.rem(row + step, row_count)
        res, ims = [], []
        for lead in range(RADIX):
            data = jnp.concatenate(
                [
                    jnp.concatenate(
                        [
                            part[0, block, kind, :, lead * half : (lead + 1) * half],
                            other[block, kind, :, lead * half : (lead + 1) * half],
                        ],
                        axis=1,
                    )
                    for kind in range(2)
                ],
                axis=0,
            )
            broad = data.shape[1]
            both = dot32(data, time[lead, :broad]) + dot32(data, time[lead, broad:])
            res.append(both[:count, :broad] - both[count:, broad:])
            ims.append(both[:count, broad:] + both[count:, :broad])
        out_re, out_im = butterfly(res, ims)
        for kind, values in ((0, out_re), (1, out_im)):
            for quarter in range(RADIX):
                ready = (values[quarter] * scale).astype(stage.dtype)
                for at in range(deep):
                    stage[block, at, kind, :, quarter * broad : (quarter + 1) * broad] = ready[
                        at * span : (at + 1) * span
                    ]
        for turn in range(1, deep):
            out_copy(step, turn).start()

        @pl.when(step != 0)
        def _():
            out_copy(step, 0).start()

        @pl.when(step == 0)
        def _():
            local.start()

    local.wait()
    for step, turn in turns:
        out_copy(step, turn).wait()


def work(tiles, near, far, pick_h, order, flip, freq_table, time_table, scale, deep):
    row_count, col_count, size, _ = tiles.shape
    length = row_count * time_table.shape[-1] // 2
    rows = freq_table.shape[-2]
    width = row_count * size
    span = rows // deep
    count = RADIX * deep
    bf16 = jnp.bfloat16
    tiles = tiles.reshape(row_count, row_count, CORES, size, size)
    small = [near, far, pick_h, order, flip]
    return pl.pallas_call(
        lambda *refs: plane_kernel(scale, *refs),
        out_shape=jax.ShapeDtypeStruct((count, 2, span, length), bf16),
        in_specs=[pl.BlockSpec(memory_space=pl.ANY)]
        + [pl.BlockSpec(memory_space=pltpu.VMEM)] * len(small)
        + [pl.BlockSpec(memory_space=pl.ANY)] * 2,
        out_specs=pl.BlockSpec(memory_space=pl.ANY),
        scratch_shapes=[
            pltpu.VMEM(tiles.shape, tiles.dtype),
            pltpu.VMEM((row_count, row_count, size, size), tiles.dtype),
            pltpu.VMEM((RADIX, length // RADIX, width), bf16),
            pltpu.VMEM(freq_table.shape, bf16),
            pltpu.VMEM(time_table.shape, bf16),
            pltpu.VMEM((CORES, RADIX, 2, rows, width), bf16),
            pltpu.VMEM((RADIX, 2, rows, width), bf16),
            pltpu.VMEM((RADIX, deep, 2, span, length), bf16),
            pltpu.SemaphoreType.DMA((4,)),
            pltpu.SemaphoreType.DMA((4,)),
            pltpu.SemaphoreType.DMA((count,)),
            pltpu.SemaphoreType.DMA((count,)),
        ],
        compiler_params=pltpu.CompilerParams(
            collective_id=0, has_side_effects=True, vmem_limit_bytes=LIMIT
        ),
        cost_estimate=pl.CostEstimate(
            flops=70 * 10**9, bytes_accessed=10**7, transcendentals=0
        ),
    )(tiles, *small, freq_table, time_table)


def widen_kernel(got_ref, *refs):
    re_ref, im_ref = refs[-2:]
    re_ref[...] = got_ref[:, 0].astype(jnp.float32)
    im_ref[...] = got_ref[:, 1].astype(jnp.float32)


def widen(at, rounds, received, outs):
    count, _, rows, length = received.shape
    lot = 2
    shape = jax.ShapeDtypeStruct((rounds * count, rows, length), jnp.float32)
    spec = pl.BlockSpec((lot, rows, length), lambda c: (at * (count // lot) + c, 0, 0))
    return pl.pallas_call(
        widen_kernel,
        out_shape=(shape, shape),
        grid=(count // lot,),
        in_specs=[pl.BlockSpec((lot, 2, rows, length), lambda c: (c, 0, 0, 0))]
        + [pl.BlockSpec(memory_space=pl.ANY)] * len(outs),
        out_specs=(spec, spec),
        input_output_aliases={1 + which: which for which in range(len(outs))},
        compiler_params=pltpu.CompilerParams(vmem_limit_bytes=LIMIT),
        cost_estimate=pl.CostEstimate(
            flops=8 * 10**9, bytes_accessed=received.size * 6, transcendentals=0
        ),
    )(received, *outs)


def plane_body(intensity, punch_radius):
    row_count = lax.axis_size("row")
    col_count = lax.axis_size("col")
    row = lax.axis_index("row")
    col = lax.axis_index("col")
    core = col % CORES
    deep = col_count // (HALVES * CORES)
    layer = col // CORES % deep
    half = col // (CORES * deep)
    planes, h_block, size = intensity.shape
    length = h_block * row_count
    width = length // RADIX
    lot = row_count * deep
    rounds = planes // lot
    span = length // (row_count * col_count)
    bf16 = jnp.bfloat16

    node_count = punch_radius.shape[1]
    node_ids = jnp.arange(node_count, dtype=jnp.int32)
    whole = jnp.arange(length, dtype=jnp.int32)
    inner = jnp.arange(size, dtype=jnp.int32)
    tile_rows = jnp.arange(row_count, dtype=jnp.int32)
    pick_k = ((whole[:, None] + SP // 2) // SP == node_ids[None, :]).astype(bf16)
    mine = ((CORES * tile_rows + core)[:, None] * size + inner[None, :]).reshape(-1)
    pick_h = ((mine[None, :] + SP // 2) // SP == node_ids[:, None]).astype(bf16)

    def limits(at):
        level = at * lot + row * deep + layer
        node = (level + SP // 2) // SP
        off = level - SP * node
        table = lax.dynamic_index_in_dim(punch_radius, node, 0, keepdims=False) - off * off
        table = table.astype(bf16)
        near = jnp.einsum("kn,nm->km", pick_k, table, preferred_element_type=jnp.float32)
        far = jnp.einsum("kn,mn->km", pick_k, table, preferred_element_type=jnp.float32)
        return near.astype(bf16), far.astype(bf16)

    local = jnp.arange(size, dtype=jnp.int32)
    source = RADIX * (local % (size // RADIX)) + local // (size // RADIX)
    order = (source[:, None] == local[None, :]).astype(bf16)
    wide = jnp.arange(2 * size, dtype=jnp.int32)
    lead_of = wide // (2 * size // RADIX)
    tile_of = wide // (size // RADIX) % 2
    from_wide = tile_of * size + RADIX * (wide % (size // RADIX)) + lead_of
    flip = (from_wide[None, :] == wide[:, None]).astype(bf16)

    fine = 16
    lead_ids = jnp.arange(RADIX, dtype=jnp.int32)
    low_ids = jnp.arange(fine, dtype=jnp.int32)
    minor = jnp.arange(width, dtype=jnp.int32)
    sides = jnp.stack([core, 1 - core])
    layers = jnp.arange(deep, dtype=jnp.int32)
    starts = (
        half * (width // HALVES)
        + CORES * span * layers[None, :, None]
        + span * sides[:, None, None]
        + fine * jnp.arange(span // fine, dtype=jnp.int32)[None, None, :]
    ).reshape(-1)
    sample = RADIX * minor[None, None, None, :] + lead_ids[:, None, None, None]
    freq = packed(
        spin(sample, starts[None, :, None, None], length),
        spin(sample, low_ids[None, None, :, None], length),
        (RADIX, CORES, 1, deep * span, width),
    )
    freq_table = jnp.stack(halves(jnp.concatenate(freq, axis=2))).reshape(
        2, RADIX, CORES, 2, deep * span, width
    )
    piece = size // RADIX
    blocks = (
        piece * (CORES * tile_rows[None, :, None] + sides[:, None, None])
        + fine * jnp.arange(piece // fine, dtype=jnp.int32)[None, None, :]
    ).reshape(-1)
    time = packed(
        spin(RADIX * blocks[None, :, None, None], minor, length),
        spin(RADIX * low_ids[None, None, :, None] + lead_ids[:, None, None, None], minor, length),
        (RADIX, width, width),
    )
    time_table = jnp.concatenate(halves(jnp.concatenate(time, axis=2)), axis=1)

    order_like = (row_count, 1, deep, CORES, size, size)

    def spread(at):
        block = intensity[at * lot : (at + 1) * lot]
        coded = encode(block).reshape(order_like)
        both = jnp.broadcast_to(coded, (row_count, HALVES) + order_like[2:])
        return both.reshape(-1, size, size)

    def gather(sent):
        return lax.all_to_all(sent, ("row", "col"), split_axis=0, concat_axis=0, tiled=True)

    coming = gather(spread(0))
    bounds = [limits(at) for at in range(rounds)]
    waiting = [spread(at) for at in range(1, rounds)]
    waiting, bounds, freq_table, time_table, pick_h, order, flip = lax.optimization_barrier(
        (waiting, bounds, freq_table, time_table, pick_h, order, flip)
    )
    outs = ()

    for at in range(rounds):
        tiles = coming
        if at + 1 < rounds:
            coming = gather(waiting[at])
        received = work(
            tiles.reshape(row_count, col_count, size, size),
            *bounds[at],
            pick_h,
            order,
            flip,
            freq_table,
            time_table,
            1.0 / length,
            deep,
        )
        if at + 1 < rounds:
            received, coming = lax.optimization_barrier((received, coming))
        outs = widen(at, rounds, received, outs)
    return outs


def body(intensity, punch_radius):
    row_count = lax.axis_size("row")
    col_count = lax.axis_size("col")
    planes, _, k_block = intensity.shape
    by_plane = row_count == RADIX and col_count == HALVES * RADIX
    by_plane = by_plane and planes % (row_count * col_count // RADIX) == 0 and k_block % 256 == 0
    return (plane_body if by_plane else pencil_body)(intensity, punch_radius)


def solution(mesh):
    in_specs = (P(None, "row", "col"), P())
    out_specs = (P(None, ("row", "col"), None), P(None, ("row", "col"), None))
    return jax.shard_map(body, mesh=mesh, in_specs=in_specs, out_specs=out_specs, check_vma=False)
```

```python
import math

import jax
import jax.numpy as jnp
from jax import lax
from jax.experimental import pallas as pl
from jax.experimental.pallas import tpu as pltpu
from jax.sharding import PartitionSpec as P

N = 2048
SP = 16


def circle(count, period, width):
    first_ids = jnp.arange(count, dtype=jnp.int32)
    second_ids = jnp.arange(width, dtype=jnp.int32)
    phases = first_ids[:, None] * second_ids[None, :] % period
    angles = phases.astype(jnp.float32) * (2.0 * math.pi / period)
    return (jnp.cos(angles), jnp.sin(angles))


def mixed(form, left, right):
    return jnp.einsum(form, left, right, precision=lax.Precision.HIGHEST)


def spectral(real_in, imag_in):
    length = real_in.shape[-1]
    first = 32
    second = length // first
    shape_lead = real_in.shape[:-1]
    cos_first, sin_first = circle(first, first, first)
    cos_twist, sin_twist = circle(first, length, second)
    cos_second, sin_second = circle(second, second, second)
    grid_re = real_in.reshape(shape_lead + (first, second))
    section_re = mixed("...ab,ac->...cb", grid_re, cos_first)
    section_im = mixed("...ab,ac->...cb", grid_re, sin_first)
    grid_im = imag_in.reshape(shape_lead + (first, second))
    section_re = section_re - mixed("...ab,ac->...cb", grid_im, sin_first)
    section_im = section_im + mixed("...ab,ac->...cb", grid_im, cos_first)
    twist_re = section_re * cos_twist - section_im * sin_twist
    twist_im = section_re * sin_twist + section_im * cos_twist
    final_re = mixed("...cb,bd->...dc", twist_re, cos_second) - mixed(
        "...cb,bd->...dc", twist_im, sin_second
    )
    final_im = mixed("...cb,bd->...dc", twist_re, sin_second) + mixed(
        "...cb,bd->...dc", twist_im, cos_second
    )
    return (final_re.reshape(shape_lead + (length,)), final_im.reshape(shape_lead + (length,)))


def spectral_lead(real_in):
    row_total, length = real_in.shape
    first = 32
    second = length // first
    cos_first, sin_first = circle(first, first, first)
    cos_twist, sin_twist = circle(first, length, second)
    cos_second, sin_second = circle(second, second, second)
    grid_re = real_in.reshape(row_total, first, second)
    section_re = mixed("rab,ac->cbr", grid_re, cos_first)
    section_im = mixed("rab,ac->cbr", grid_re, sin_first)
    twist_re = section_re * cos_twist[:, :, None] - section_im * sin_twist[:, :, None]
    twist_im = section_re * sin_twist[:, :, None] + section_im * cos_twist[:, :, None]
    final_re = mixed("cbr,bd->dcr", twist_re, cos_second) - mixed(
        "cbr,bd->dcr", twist_im, sin_second
    )
    final_im = mixed("cbr,bd->dcr", twist_re, sin_second) + mixed(
        "cbr,bd->dcr", twist_im, cos_second
    )
    return (final_re.reshape(length, row_total), final_im.reshape(length, row_total))


def keep_map(first_coords, second_coords, radius_table, levels):
    node_count = radius_table.shape[1]
    first_node = (first_coords + SP // 2) // SP
    first_dist = first_coords - SP * first_node
    second_node = (second_coords + SP // 2) // SP
    second_dist = second_coords - SP * second_node
    plane_node = (levels + SP // 2) // SP
    plane_dist = levels - SP * plane_node
    node_ids = jnp.arange(node_count, dtype=jnp.int32)
    pick_first = (first_node[:, None] == node_ids[None, :]).astype(jnp.bfloat16)
    pick_second = (second_node[:, None] == node_ids[None, :]).astype(jnp.bfloat16)
    table_half = jnp.einsum(
        "hn,snm->shm",
        pick_first,
        radius_table.astype(jnp.bfloat16),
        preferred_element_type=jnp.float32,
    ).astype(jnp.bfloat16)
    plane_radius = jnp.einsum(
        "shm,km->shk", table_half, pick_second, preferred_element_type=jnp.float32
    )
    level_ids = jnp.arange(radius_table.shape[0], dtype=jnp.int32)
    pick_plane = (plane_node[:, None] == level_ids[None, :]).astype(jnp.float32)
    radius = jnp.einsum("ls,shk->hlk", pick_plane, plane_radius, precision=lax.Precision.HIGHEST)
    distance = (
        (first_dist * first_dist)[:, None, None]
        + (plane_dist * plane_dist)[None, :, None]
        + (second_dist * second_dist)[None, None, :]
    )
    return (distance.astype(jnp.float32) >= radius).astype(jnp.float32)


def pencil_body(intensity, punch_radius):
    row_count = lax.axis_size("row")
    col_count = lax.axis_size("col")
    row_at = lax.axis_index("row")
    col_at = lax.axis_index("col")
    planes, h_block, k_block = intensity.shape
    groups = col_count // row_count
    fine_width = k_block // col_count
    pencil_rows = groups * fine_width
    levels = jnp.arange(planes, dtype=jnp.int32)
    swapped_table = jnp.swapaxes(punch_radius, 1, 2)
    outgoing = jnp.transpose(
        intensity.reshape(planes, h_block, col_count, fine_width), (2, 3, 0, 1)
    )
    arrived = lax.all_to_all(
        lax.all_to_all(outgoing, "col", split_axis=0, concat_axis=0, tiled=True),
        "row",
        split_axis=0,
        concat_axis=3,
        tiled=True,
    )
    pencil_h = (
        h_block * row_at
        + k_block * jnp.arange(groups, dtype=jnp.int32)[:, None]
        + fine_width * col_at
        + jnp.arange(fine_width, dtype=jnp.int32)[None, :]
    ).reshape(-1)
    whole_k = jnp.arange(N, dtype=jnp.int32)
    mirrored = arrived.reshape(pencil_rows, planes, N)
    pencil_input = jnp.transpose(
        intensity.reshape(planes, groups, col_count, fine_width, k_block), (1, 2, 3, 0, 4)
    )
    direct = lax.all_to_all(pencil_input, "col", split_axis=1, concat_axis=4, tiled=True).reshape(
        pencil_rows, planes, N
    )
    keep_mask = keep_map(pencil_h, whole_k, punch_radius, levels)
    keep_swap = keep_map(pencil_h, whole_k, swapped_table, levels)
    counts = jnp.maximum(keep_mask + keep_swap, 1.0)
    symmetric = ((keep_mask * direct + keep_swap * mirrored) / counts).astype(jnp.bfloat16)
    row_total = pencil_rows * planes
    flat_rows = symmetric.reshape(row_total, N).astype(jnp.float32)
    part_re, part_im = spectral_lead(flat_rows)
    freq_width = N // (row_count * col_count)
    sectioned = jnp.stack([part_re, part_im]).reshape(
        2, row_count, col_count, freq_width, row_total
    )
    spectra = lax.all_to_all(
        lax.all_to_all(sectioned, "row", split_axis=1, concat_axis=1, tiled=True),
        "col",
        split_axis=2,
        concat_axis=2,
        tiled=True,
    )
    spectra = spectra.reshape(2, row_count, col_count, freq_width, groups, fine_width, planes)
    spectra = jnp.transpose(spectra, (0, 6, 3, 1, 4, 2, 5)).reshape(2, planes * freq_width, N)
    final_re, final_im = spectral(spectra[0], spectra[1])
    out_re = (final_re / N).reshape(planes, freq_width, N)
    out_im = (final_im / N).reshape(planes, freq_width, N)
    return (out_re, out_im)


RADIX = 4
HALVES = 2
CORES = 2
CURVE = 7
CODE_BITS = 102
UNIT = 2.0**-CODE_BITS
LIMIT = 60 * 1024 * 1024


def spin(first_ids, second_ids, period):
    phases = first_ids * second_ids % period
    angles = phases.astype(jnp.float32) * (2.0 * math.pi / period)
    return jnp.cos(angles), jnp.sin(angles)


def halves(values):
    high = lax.reduce_precision(values, exponent_bits=8, mantissa_bits=7)
    return high.astype(jnp.bfloat16), (values - high).astype(jnp.bfloat16)


def packed(coarse, fine, shape):
    coarse_re, coarse_im = coarse
    fine_re, fine_im = fine
    full_re = (coarse_re * fine_re - coarse_im * fine_im).reshape(shape)
    full_im = (coarse_re * fine_im + coarse_im * fine_re).reshape(shape)
    return full_re, full_im


def dot32(left, right):
    return jnp.dot(left, right, preferred_element_type=jnp.float32)


def butterfly(res, ims):
    even_re, odd_re = res[0] + res[2], res[0] - res[2]
    even_im, odd_im = ims[0] + ims[2], ims[0] - ims[2]
    pair_re, gap_re = res[1] + res[3], res[1] - res[3]
    pair_im, gap_im = ims[1] + ims[3], ims[1] - ims[3]
    out_re = (even_re + pair_re, odd_re - gap_im, even_re - pair_re, odd_re + gap_im)
    out_im = (even_im + pair_im, odd_im + gap_re, even_im - pair_im, odd_im - gap_re)
    return out_re, out_im


def encode(values):
    size = jnp.exp2(jnp.log2(jnp.abs(values)) * (1.0 / CURVE)) * 2.0 ** (CODE_BITS / CURVE)
    return jnp.where(values < 0, -jnp.round(size), jnp.round(size)).astype(jnp.int32).astype(jnp.int16)


def decode(codes):
    base = codes.astype(jnp.int32).astype(jnp.float32)
    square = base * base
    return (square * square) * (square * base)


def keep_scale(near, far, picked, distance):
    keep_mirror = distance >= dot32(near, picked)
    keep_direct = distance >= dot32(far, picked)
    scale = jnp.where(keep_mirror & keep_direct, 0.5 * UNIT, UNIT)
    return jnp.where(keep_mirror, scale, 0.0), jnp.where(keep_direct, scale, 0.0)


def encode_kernel(values_ref, codes_ref):
    codes = encode(values_ref[0])
    codes = codes.reshape(codes_ref.shape[3:])
    for half in range(HALVES):
        codes_ref[0, half, 0] = codes


def encode_first(intensity, lot, deep):
    _, h_block, size = intensity.shape
    rows = lot // deep
    return pl.pallas_call(
        encode_kernel,
        out_shape=jax.ShapeDtypeStruct((rows, HALVES, deep, CORES, size, size), jnp.int16),
        grid=(lot,),
        in_specs=[pl.BlockSpec((1, h_block, size), lambda p: (p, 0, 0))],
        out_specs=pl.BlockSpec(
            (1, HALVES, 1, CORES, size, size), lambda p: (p // deep, 0, p % deep, 0, 0, 0)
        ),
    )(intensity)


def plane_kernel(
    scale,
    first_ref,
    codes_ref,
    near_ref,
    far_ref,
    pick_ref,
    order_ref,
    flip_ref,
    freq_hbm,
    time_hbm,
    got_ref,
    tiles,
    mirror,
    sym,
    freq,
    time,
    part,
    other,
    stage,
    load_sem,
    in_send,
    in_recv,
    swap_sem,
    out_send,
    out_recv,
):
    row_count = lax.axis_size("row")
    col_count = lax.axis_size("col")
    row = lax.axis_index("row")
    col = lax.axis_index("col")
    core = lax.rem(col, CORES)
    deep, span = stage.shape[1], stage.shape[3]
    size = tiles.shape[-1]
    layer = lax.rem(col // CORES, deep)
    base = col - core - CORES * layer
    mine = row * deep + layer
    lot = row_count * deep
    me = row * col_count + col
    devices = row_count * col_count
    twin = {"col": col + 1 - 2 * core}

    loads = [
        pltpu.make_async_copy(first_ref, tiles.at[0], load_sem.at[0]),
        pltpu.make_async_copy(freq_hbm, freq, load_sem.at[1]),
        pltpu.make_async_copy(time_hbm, time, load_sem.at[2]),
    ]
    for load in loads:
        load.start()

    def device(place):
        return {"row": place // col_count, "col": lax.rem(place, col_count)}

    barrier = pltpu.get_barrier_semaphore()

    @pl.loop(1, devices)
    def _(step):
        pl.semaphore_signal(barrier, inc=1, device_id=device(lax.rem(me + step, devices)))

    pl.semaphore_wait(barrier, devices - 1)

    def swap(turn, source):
        return pltpu.make_async_remote_copy(
            src_ref=source,
            dst_ref=mirror.at[turn],
            send_sem=swap_sem.at[turn, 0],
            recv_sem=swap_sem.at[turn, 1],
            device_id=twin,
        )

    def trade(turn):
        return pltpu.make_async_remote_copy(
            src_ref=part.at[1],
            dst_ref=other.at[turn],
            send_sem=swap_sem.at[turn, 2],
            recv_sem=swap_sem.at[turn, 3],
            device_id=twin,
        )

    swaps = [
        swap(0, first_ref.at[:, :, 1 - core]),
        swap(1, tiles.at[1, :, :, 1 - core]),
    ]
    swaps[0].start()

    def in_copy(target, source):
        to_row = target // col_count
        to_col = lax.rem(target, col_count)
        from_row = source // col_count
        from_col = lax.rem(source, col_count)
        return pltpu.make_async_remote_copy(
            src_ref=codes_ref.at[
                to_row, lax.rem(to_col // CORES, deep), lax.rem(to_col, CORES)
            ],
            dst_ref=tiles.at[1, from_row, from_col // CORES, lax.rem(from_col, CORES)],
            send_sem=in_send.at[target],
            recv_sem=in_recv.at[source],
            device_id=device(target),
        )

    @pl.loop(1, devices)
    def _(step):
        in_copy(lax.rem(me + step, devices), me).start()

    inside = pltpu.make_async_copy(
        codes_ref.at[row, layer, core], tiles.at[1, row, col // CORES, core], load_sem.at[3]
    )
    inside.start()

    width = 2 * size
    piece = width // RADIX
    pairs = row_count // 2
    rows = lax.broadcasted_iota(jnp.int32, (size, width), 0)
    cols = lax.broadcasted_iota(jnp.int32, (size, width), 1)
    row_off = (rows + SP // 2) % SP - SP // 2
    col_off = (cols + SP // 2) % SP - SP // 2
    distance = (row_off * row_off + col_off * col_off).astype(jnp.float32)

    def blend(turn, block, parity, reflected):
        at = pl.multiple_of((CORES * block + parity) * size, size)
        for pair in range(pairs):
            picked = pick_ref[:, pair * width : (pair + 1) * width]
            by_mirror, by_direct = keep_scale(
                near_ref[turn, pl.ds(at, size)], far_ref[turn, pl.ds(at, size)], picked, distance
            )
            turned = jnp.concatenate(
                [decode(tiles[turn, 2 * pair + up, block, parity]).T for up in range(2)], axis=1
            )
            across = jnp.concatenate(
                [decode(reflected(block, 2 * pair + up)) for up in range(2)], axis=1
            )
            total = by_mirror * across + by_direct * turned
            half = dot32(order_ref[...], total.astype(jnp.bfloat16)).astype(jnp.bfloat16)
            ready = dot32(half, flip_ref[...]).astype(jnp.bfloat16)
            ready = ready.reshape(RADIX, size // RADIX, width)
            spot = pl.multiple_of((CORES * block + parity) * (size // RADIX), size // RADIX)
            for lead in range(RADIX):
                start = (lead * pairs + pair) * piece
                sym[:, pl.ds(spot, size // RADIX), start : start + piece] = ready[
                    :, :, lead * piece : (lead + 1) * piece
                ]

    def blend_all(turn):
        @pl.loop(0, row_count)
        def _(block):
            blend(turn, block, core, lambda at, up: tiles[turn, at, up, core])

        swaps[turn].wait()

        @pl.loop(0, row_count)
        def _(block):
            blend(turn, block, 1 - core, lambda at, up: mirror[turn, at, up])

    count = part.shape[3]

    def first_all(turn):
        for side in (1, 0):
            res, ims = [], []
            for lead in range(RADIX):
                data = sym[lead]
                high = freq[0, lead, side].reshape(2 * count, -1)
                low = freq[1, lead, side].reshape(2 * count, -1)
                both = dot32(high, data) + dot32(low, data)
                res.append(both[:count])
                ims.append(both[count:])
            out_re, out_im = butterfly(res, ims)
            for block in range(RADIX):
                part[side, block, 0] = out_re[block].astype(part.dtype)
                part[side, block, 1] = out_im[block].astype(part.dtype)
            if side:
                trade(turn).start()

    def out_copy(turn, step, shift):
        to_row = lax.rem(row + step, row_count)
        to_layer = lax.rem(layer + shift, deep)
        return pltpu.make_async_remote_copy(
            src_ref=stage.at[to_row, to_layer],
            dst_ref=got_ref.at[turn, mine],
            send_sem=out_send.at[turn, step * deep + shift],
            recv_sem=out_recv.at[turn, step * deep + shift],
            device_id={"row": to_row, "col": base + CORES * to_layer + core},
        )

    def own(turn):
        return pltpu.make_async_copy(
            stage.at[row, layer], got_ref.at[turn, mine], out_recv.at[turn, 0]
        )

    half = part.shape[-1] // RADIX

    def second_all(turn):
        @pl.loop(0, row_count)
        def _(tick):
            step = lax.rem(tick + 1, row_count)
            block = lax.rem(row + step, row_count)
            res, ims = [], []
            for lead in range(RADIX):
                data = jnp.concatenate(
                    [
                        jnp.concatenate(
                            [
                                part[0, block, kind, :, lead * half : (lead + 1) * half],
                                other[turn, block, kind, :, lead * half : (lead + 1) * half],
                            ],
                            axis=1,
                        )
                        for kind in range(2)
                    ],
                    axis=0,
                )
                broad = data.shape[1]
                both = dot32(data, time[lead, :broad]) + dot32(data, time[lead, broad:])
                res.append(both[:count, :broad] - both[count:, broad:])
                ims.append(both[:count, broad:] + both[count:, :broad])
            out_re, out_im = butterfly(res, ims)
            for kind, values in ((0, out_re), (1, out_im)):
                for quarter in range(RADIX):
                    ready = (values[quarter] * scale).astype(stage.dtype)
                    for at in range(deep):
                        stage[block, at, kind, :, quarter * broad : (quarter + 1) * broad] = (
                            ready[at * span : (at + 1) * span]
                        )
            for shift in range(1, deep):
                out_copy(turn, step, shift).start()

            @pl.when(step != 0)
            def _():
                out_copy(turn, step, 0).start()

            @pl.when(step == 0)
            def _():
                own(turn).start()

    loads[0].wait()
    blend_all(0)
    loads[1].wait()
    first_all(0)
    loads[2].wait()
    trade(0).wait()
    second_all(0)
    inside.wait()

    @pl.loop(1, devices)
    def _(step):
        in_copy(me, lax.rem(me + step, devices)).wait_recv()

    swaps[1].start()
    blend_all(1)
    first_all(1)
    trade(1).wait()
    for at in range(1, lot):
        out_copy(0, at // deep, at % deep).wait_send()
    own(0).wait()
    second_all(1)
    own(1).wait()
    for turn in range(2):
        for at in range(1, lot):
            out_copy(turn, at // deep, at % deep).wait_recv()
    for at in range(1, lot):
        out_copy(1, at // deep, at % deep).wait_send()

    @pl.loop(1, devices)
    def _(step):
        in_copy(lax.rem(me + step, devices), me).wait_send()


def work(tiles, codes, near, far, pick_h, order, flip, freq_table, time_table, scale, deep):
    row_count, _, _, size, _ = tiles.shape
    devices = row_count * tiles.shape[1] * CORES
    length = row_count * time_table.shape[-1] // 2
    rows = freq_table.shape[-2]
    width = row_count * size
    span = rows // deep
    lot = row_count * deep
    bf16 = jnp.bfloat16
    small = [near, far, pick_h, order, flip]
    return pl.pallas_call(
        lambda *refs: plane_kernel(scale, *refs),
        out_shape=jax.ShapeDtypeStruct((2, lot, 2, span, length), bf16),
        in_specs=[pl.BlockSpec(memory_space=pl.ANY)] * 2
        + [pl.BlockSpec(memory_space=pltpu.VMEM)] * len(small)
        + [pl.BlockSpec(memory_space=pl.ANY)] * 2,
        out_specs=pl.BlockSpec(memory_space=pl.ANY),
        scratch_shapes=[
            pltpu.VMEM((2,) + tiles.shape, tiles.dtype),
            pltpu.VMEM((2, row_count, row_count, size, size), tiles.dtype),
            pltpu.VMEM((RADIX, length // RADIX, width), bf16),
            pltpu.VMEM(freq_table.shape, bf16),
            pltpu.VMEM(time_table.shape, bf16),
            pltpu.VMEM((CORES, RADIX, 2, rows, width), bf16),
            pltpu.VMEM((2, RADIX, 2, rows, width), bf16),
            pltpu.VMEM((RADIX, deep, 2, span, length), bf16),
            pltpu.SemaphoreType.DMA((4,)),
            pltpu.SemaphoreType.DMA((devices,)),
            pltpu.SemaphoreType.DMA((devices,)),
            pltpu.SemaphoreType.DMA((2, 4)),
            pltpu.SemaphoreType.DMA((2, lot)),
            pltpu.SemaphoreType.DMA((2, lot)),
        ],
        compiler_params=pltpu.CompilerParams(
            collective_id=0, has_side_effects=True, vmem_limit_bytes=LIMIT
        ),
        cost_estimate=pl.CostEstimate(
            flops=140 * 10**9, bytes_accessed=10**7, transcendentals=0
        ),
    )(tiles, codes, *small, freq_table, time_table)


def widen_kernel(got_ref, re_ref, im_ref):
    re_ref[...] = got_ref[:, 0].astype(jnp.float32)
    im_ref[...] = got_ref[:, 1].astype(jnp.float32)


def widen(got):
    count, _, span, length = got.shape
    spec = pl.BlockSpec((1, span, length), lambda at: (at, 0, 0))
    shape = jax.ShapeDtypeStruct((count, span, length), jnp.float32)
    return pl.pallas_call(
        widen_kernel,
        out_shape=(shape, shape),
        grid=(count,),
        in_specs=[pl.BlockSpec((1, 2, span, length), lambda at: (at, 0, 0, 0))],
        out_specs=(spec, spec),
    )(got)


def plane_body(intensity, punch_radius):
    row_count = lax.axis_size("row")
    col_count = lax.axis_size("col")
    row = lax.axis_index("row")
    col = lax.axis_index("col")
    core = col % CORES
    deep = col_count // (HALVES * CORES)
    layer = col // CORES % deep
    half = col // (CORES * deep)
    planes, h_block, size = intensity.shape
    length = h_block * row_count
    width = length // RADIX
    lot = row_count * deep
    span = length // (row_count * col_count)
    bf16 = jnp.bfloat16

    node_count = punch_radius.shape[1]
    node_ids = jnp.arange(node_count, dtype=jnp.int32)
    whole = jnp.arange(length, dtype=jnp.int32)
    inner = jnp.arange(size, dtype=jnp.int32)
    tile_rows = jnp.arange(row_count, dtype=jnp.int32)
    pick_k = ((whole[:, None] + SP // 2) // SP == node_ids[None, :]).astype(bf16)
    mine = ((CORES * tile_rows + core)[:, None] * size + inner[None, :]).reshape(-1)
    pick_h = ((mine[None, :] + SP // 2) // SP == node_ids[:, None]).astype(bf16)

    def limits(at):
        level = at * lot + row * deep + layer
        node = (level + SP // 2) // SP
        off = level - SP * node
        table = lax.dynamic_index_in_dim(punch_radius, node, 0, keepdims=False) - off * off
        table = table.astype(bf16)
        near = jnp.einsum("kn,nm->km", pick_k, table, preferred_element_type=jnp.float32)
        far = jnp.einsum("kn,mn->km", pick_k, table, preferred_element_type=jnp.float32)
        return near.astype(bf16), far.astype(bf16)

    local = jnp.arange(size, dtype=jnp.int32)
    source = RADIX * (local % (size // RADIX)) + local // (size // RADIX)
    order = (source[:, None] == local[None, :]).astype(bf16)
    wide = jnp.arange(2 * size, dtype=jnp.int32)
    lead_of = wide // (2 * size // RADIX)
    tile_of = wide // (size // RADIX) % 2
    from_wide = tile_of * size + RADIX * (wide % (size // RADIX)) + lead_of
    flip = (from_wide[None, :] == wide[:, None]).astype(bf16)

    fine = 16
    lead_ids = jnp.arange(RADIX, dtype=jnp.int32)
    low_ids = jnp.arange(fine, dtype=jnp.int32)
    minor = jnp.arange(width, dtype=jnp.int32)
    sides = jnp.stack([core, 1 - core])
    layers = jnp.arange(deep, dtype=jnp.int32)
    starts = (
        half * (width // HALVES)
        + CORES * span * layers[None, :, None]
        + span * sides[:, None, None]
        + fine * jnp.arange(span // fine, dtype=jnp.int32)[None, None, :]
    ).reshape(-1)
    sample = RADIX * minor[None, None, None, :] + lead_ids[:, None, None, None]
    freq = packed(
        spin(sample, starts[None, :, None, None], length),
        spin(sample, low_ids[None, None, :, None], length),
        (RADIX, CORES, 1, deep * span, width),
    )
    freq_table = jnp.stack(halves(jnp.concatenate(freq, axis=2))).reshape(
        2, RADIX, CORES, 2, deep * span, width
    )
    piece = size // RADIX
    blocks = (
        piece * (CORES * tile_rows[None, :, None] + sides[:, None, None])
        + fine * jnp.arange(piece // fine, dtype=jnp.int32)[None, None, :]
    ).reshape(-1)
    time = packed(
        spin(RADIX * blocks[None, :, None, None], minor, length),
        spin(RADIX * low_ids[None, None, :, None] + lead_ids[:, None, None, None], minor, length),
        (RADIX, width, width),
    )
    time_table = jnp.concatenate(halves(jnp.concatenate(time, axis=2)), axis=1)

    sent = encode_first(intensity, lot, deep).reshape(-1, size, size)
    tiles = lax.all_to_all(sent, ("row", "col"), split_axis=0, concat_axis=0, tiled=True)
    codes = encode(intensity[lot:]).reshape(row_count, deep, CORES, size, size)
    near, far = (jnp.stack(pair) for pair in zip(*(limits(at) for at in range(2))))
    got = work(
        tiles.reshape(row_count, row_count, CORES, size, size),
        codes,
        near,
        far,
        pick_h,
        order,
        flip,
        freq_table,
        time_table,
        1.0 / length,
        deep,
    )
    return tuple(widen(got.reshape((planes,) + got.shape[2:])))


def body(intensity, punch_radius):
    row_count = lax.axis_size("row")
    col_count = lax.axis_size("col")
    planes, _, k_block = intensity.shape
    by_plane = row_count == RADIX and col_count == HALVES * RADIX
    by_plane = by_plane and 2 * planes == row_count * col_count and k_block % 256 == 0
    return (plane_body if by_plane else pencil_body)(intensity, punch_radius)


def solution(mesh):
    in_specs = (P(None, "row", "col"), P())
    out_specs = (P(None, ("row", "col"), None), P(None, ("row", "col"), None))
    return jax.shard_map(body, mesh=mesh, in_specs=in_specs, out_specs=out_specs, check_vma=False)
```

```python
import math

import jax
import jax.numpy as jnp
import numpy as np
from jax import lax
from jax.experimental import pallas as pl
from jax.experimental.pallas import tpu as pltpu
from jax.sharding import PartitionSpec as P

N = 2048
SP = 16


def circle(count, period, width):
    first_ids = jnp.arange(count, dtype=jnp.int32)
    second_ids = jnp.arange(width, dtype=jnp.int32)
    phases = first_ids[:, None] * second_ids[None, :] % period
    angles = phases.astype(jnp.float32) * (2.0 * math.pi / period)
    return (jnp.cos(angles), jnp.sin(angles))


def mixed(form, left, right):
    return jnp.einsum(form, left, right, precision=lax.Precision.HIGHEST)


def spectral(real_in, imag_in):
    length = real_in.shape[-1]
    first = 32
    second = length // first
    shape_lead = real_in.shape[:-1]
    cos_first, sin_first = circle(first, first, first)
    cos_twist, sin_twist = circle(first, length, second)
    cos_second, sin_second = circle(second, second, second)
    grid_re = real_in.reshape(shape_lead + (first, second))
    section_re = mixed("...ab,ac->...cb", grid_re, cos_first)
    section_im = mixed("...ab,ac->...cb", grid_re, sin_first)
    grid_im = imag_in.reshape(shape_lead + (first, second))
    section_re = section_re - mixed("...ab,ac->...cb", grid_im, sin_first)
    section_im = section_im + mixed("...ab,ac->...cb", grid_im, cos_first)
    twist_re = section_re * cos_twist - section_im * sin_twist
    twist_im = section_re * sin_twist + section_im * cos_twist
    final_re = mixed("...cb,bd->...dc", twist_re, cos_second) - mixed(
        "...cb,bd->...dc", twist_im, sin_second
    )
    final_im = mixed("...cb,bd->...dc", twist_re, sin_second) + mixed(
        "...cb,bd->...dc", twist_im, cos_second
    )
    return (final_re.reshape(shape_lead + (length,)), final_im.reshape(shape_lead + (length,)))


def spectral_lead(real_in):
    row_total, length = real_in.shape
    first = 32
    second = length // first
    cos_first, sin_first = circle(first, first, first)
    cos_twist, sin_twist = circle(first, length, second)
    cos_second, sin_second = circle(second, second, second)
    grid_re = real_in.reshape(row_total, first, second)
    section_re = mixed("rab,ac->cbr", grid_re, cos_first)
    section_im = mixed("rab,ac->cbr", grid_re, sin_first)
    twist_re = section_re * cos_twist[:, :, None] - section_im * sin_twist[:, :, None]
    twist_im = section_re * sin_twist[:, :, None] + section_im * cos_twist[:, :, None]
    final_re = mixed("cbr,bd->dcr", twist_re, cos_second) - mixed(
        "cbr,bd->dcr", twist_im, sin_second
    )
    final_im = mixed("cbr,bd->dcr", twist_re, sin_second) + mixed(
        "cbr,bd->dcr", twist_im, cos_second
    )
    return (final_re.reshape(length, row_total), final_im.reshape(length, row_total))


def keep_map(first_coords, second_coords, radius_table, levels):
    node_count = radius_table.shape[1]
    first_node = (first_coords + SP // 2) // SP
    first_dist = first_coords - SP * first_node
    second_node = (second_coords + SP // 2) // SP
    second_dist = second_coords - SP * second_node
    plane_node = (levels + SP // 2) // SP
    plane_dist = levels - SP * plane_node
    node_ids = jnp.arange(node_count, dtype=jnp.int32)
    pick_first = (first_node[:, None] == node_ids[None, :]).astype(jnp.bfloat16)
    pick_second = (second_node[:, None] == node_ids[None, :]).astype(jnp.bfloat16)
    table_half = jnp.einsum(
        "hn,snm->shm",
        pick_first,
        radius_table.astype(jnp.bfloat16),
        preferred_element_type=jnp.float32,
    ).astype(jnp.bfloat16)
    plane_radius = jnp.einsum(
        "shm,km->shk", table_half, pick_second, preferred_element_type=jnp.float32
    )
    level_ids = jnp.arange(radius_table.shape[0], dtype=jnp.int32)
    pick_plane = (plane_node[:, None] == level_ids[None, :]).astype(jnp.float32)
    radius = jnp.einsum("ls,shk->hlk", pick_plane, plane_radius, precision=lax.Precision.HIGHEST)
    distance = (
        (first_dist * first_dist)[:, None, None]
        + (plane_dist * plane_dist)[None, :, None]
        + (second_dist * second_dist)[None, None, :]
    )
    return (distance.astype(jnp.float32) >= radius).astype(jnp.float32)


def pencil_body(intensity, punch_radius):
    row_count = lax.axis_size("row")
    col_count = lax.axis_size("col")
    row_at = lax.axis_index("row")
    col_at = lax.axis_index("col")
    planes, h_block, k_block = intensity.shape
    groups = col_count // row_count
    fine_width = k_block // col_count
    pencil_rows = groups * fine_width
    levels = jnp.arange(planes, dtype=jnp.int32)
    swapped_table = jnp.swapaxes(punch_radius, 1, 2)
    outgoing = jnp.transpose(
        intensity.reshape(planes, h_block, col_count, fine_width), (2, 3, 0, 1)
    )
    arrived = lax.all_to_all(
        lax.all_to_all(outgoing, "col", split_axis=0, concat_axis=0, tiled=True),
        "row",
        split_axis=0,
        concat_axis=3,
        tiled=True,
    )
    pencil_h = (
        h_block * row_at
        + k_block * jnp.arange(groups, dtype=jnp.int32)[:, None]
        + fine_width * col_at
        + jnp.arange(fine_width, dtype=jnp.int32)[None, :]
    ).reshape(-1)
    whole_k = jnp.arange(N, dtype=jnp.int32)
    mirrored = arrived.reshape(pencil_rows, planes, N)
    pencil_input = jnp.transpose(
        intensity.reshape(planes, groups, col_count, fine_width, k_block), (1, 2, 3, 0, 4)
    )
    direct = lax.all_to_all(pencil_input, "col", split_axis=1, concat_axis=4, tiled=True).reshape(
        pencil_rows, planes, N
    )
    keep_mask = keep_map(pencil_h, whole_k, punch_radius, levels)
    keep_swap = keep_map(pencil_h, whole_k, swapped_table, levels)
    counts = jnp.maximum(keep_mask + keep_swap, 1.0)
    symmetric = ((keep_mask * direct + keep_swap * mirrored) / counts).astype(jnp.bfloat16)
    row_total = pencil_rows * planes
    flat_rows = symmetric.reshape(row_total, N).astype(jnp.float32)
    part_re, part_im = spectral_lead(flat_rows)
    freq_width = N // (row_count * col_count)
    sectioned = jnp.stack([part_re, part_im]).reshape(
        2, row_count, col_count, freq_width, row_total
    )
    spectra = lax.all_to_all(
        lax.all_to_all(sectioned, "row", split_axis=1, concat_axis=1, tiled=True),
        "col",
        split_axis=2,
        concat_axis=2,
        tiled=True,
    )
    spectra = spectra.reshape(2, row_count, col_count, freq_width, groups, fine_width, planes)
    spectra = jnp.transpose(spectra, (0, 6, 3, 1, 4, 2, 5)).reshape(2, planes * freq_width, N)
    final_re, final_im = spectral(spectra[0], spectra[1])
    out_re = (final_re / N).reshape(planes, freq_width, N)
    out_im = (final_im / N).reshape(planes, freq_width, N)
    return (out_re, out_im)


RADIX = 4
HALVES = 2
CORES = 2
CURVE = 7
CODE_BITS = 102
UNIT = 2.0**-CODE_BITS
LIMIT = 60 * 1024 * 1024


def dot32(left, right):
    return jnp.dot(left, right, preferred_element_type=jnp.float32)


def butterfly(res, ims):
    even_re, odd_re = res[0] + res[2], res[0] - res[2]
    even_im, odd_im = ims[0] + ims[2], ims[0] - ims[2]
    pair_re, gap_re = res[1] + res[3], res[1] - res[3]
    pair_im, gap_im = ims[1] + ims[3], ims[1] - ims[3]
    out_re = (even_re + pair_re, odd_re - gap_im, even_re - pair_re, odd_re + gap_im)
    out_im = (even_im + pair_im, odd_im + gap_re, even_im - pair_im, odd_im - gap_re)
    return out_re, out_im


def encode(values):
    size = jnp.exp2(jnp.log2(jnp.abs(values)) * (1.0 / CURVE)) * 2.0 ** (CODE_BITS / CURVE)
    return jnp.where(values < 0, -jnp.round(size), jnp.round(size)).astype(jnp.int32).astype(jnp.int16)


def decode(codes):
    base = codes.astype(jnp.int32).astype(jnp.float32)
    square = base * base
    return (square * square) * (square * base)


def keep_scale(near, far, picked, distance):
    keep_mirror = distance >= dot32(near, picked)
    keep_direct = distance >= dot32(far, picked)
    scale = jnp.where(keep_mirror & keep_direct, 0.5 * UNIT, UNIT)
    return jnp.where(keep_mirror, scale, 0.0), jnp.where(keep_direct, scale, 0.0)


def build_tables(freq, time, flip, pick, size, lead_refs, minor_refs, half, layer_count, core):
    coarse_re, coarse_im, fine_re, fine_im = lead_refs
    fine = fine_re.shape[1]
    _, _, _, _, rows, width = freq.shape
    runs = rows // fine
    inner = runs // layer_count

    @pl.loop(0, RADIX * CORES * runs)
    def _(at):
        lead, rest = at // (CORES * runs), lax.rem(at, CORES * runs)
        side, run = rest // runs, lax.rem(rest, runs)
        owner = core + side * (1 - 2 * core)
        start = (half * layer_count + run // inner) * CORES * inner
        start = start + owner * inner + lax.rem(run, inner)
        big_re, big_im = coarse_re[start, lead], coarse_im[start, lead]
        low_re, low_im = fine_re[lead], fine_im[lead]
        place = pl.ds(pl.multiple_of(run * fine, fine), fine)
        for kind, full in (
            (0, big_re * low_re - big_im * low_im),
            (1, big_re * low_im + big_im * low_re),
        ):
            high = full.astype(jnp.bfloat16)
            freq[0, lead, side, kind, place] = high
            freq[1, lead, side, kind, place] = (full - high.astype(jnp.float32)).astype(
                jnp.bfloat16
            )

    base_re, base_im, step_re, step_im = minor_refs
    blocks = width // fine
    tile_runs = blocks // (CORES * RADIX)

    @pl.loop(0, RADIX * blocks)
    def _(at):
        lead, run = at // blocks, lax.rem(at, blocks)
        rel, rest = run // (blocks // CORES), lax.rem(run, blocks // CORES)
        owner = core + rel * (1 - 2 * core)
        start = (CORES * (rest // tile_runs) + owner) * tile_runs + lax.rem(rest, tile_runs)
        big_re, big_im = base_re[start], base_im[start]
        low_re, low_im = step_re[lead], step_im[lead]
        for kind, full in (
            (0, big_re * low_re - big_im * low_im),
            (1, big_re * low_im + big_im * low_re),
        ):
            high = full.astype(jnp.bfloat16)
            low = (full - high.astype(jnp.float32)).astype(jnp.bfloat16)
            for level, values in ((0, high), (1, low)):
                place = pl.ds(pl.multiple_of(level * width + run * fine, fine), fine)
                time[lead, place, kind * width : (kind + 1) * width] = values

    wide = flip.shape[0]
    piece = size // RADIX
    rows = lax.broadcasted_iota(jnp.int32, (wide, wide), 0)
    cols = lax.broadcasted_iota(jnp.int32, (wide, wide), 1)
    source = cols // piece % 2 * size + RADIX * (cols % piece) + cols // (2 * piece)
    flip[...] = (source == rows).astype(jnp.float32).astype(jnp.bfloat16)
    rows = lax.broadcasted_iota(jnp.int32, pick.shape, 0)
    cols = lax.broadcasted_iota(jnp.int32, pick.shape, 1)
    coord = (cols // size * CORES + core) * size + cols % size
    pick[...] = ((coord + SP // 2) // SP == rows).astype(jnp.float32).astype(jnp.bfloat16)


def plane_kernel(scale, value_ref, bar_ref, *refs):
    lead_refs, minor_refs, refs = refs[:4], refs[4:8], refs[8:]
    got_ref, raw, codes, tiles, mirror, sym, freq, time, part, other, stage = refs[:11]
    pick_ref, mask, flip_ref, mixed = refs[11:15]
    load_sem, in_send, in_recv, swap_sem, out_send, out_recv = refs[15:]
    row_count = lax.axis_size("row")
    col_count = lax.axis_size("col")
    row = lax.axis_index("row")
    col = lax.axis_index("col")
    core = lax.rem(col, CORES)
    deep, span = stage.shape[1], stage.shape[3]
    size = tiles.shape[-1]
    layer = lax.rem(col // CORES, deep)
    base = col - core - CORES * layer
    half_at = col // (CORES * deep)
    mine = row * deep + layer
    lot = row_count * deep
    me = row * col_count + col
    devices = row_count * col_count
    twin = {"col": col + 1 - 2 * core}

    def plane_of(at):
        return at // lot * lot + lax.rem(mine + lax.rem(at, lot), lot)

    def load(at):
        slot = lax.rem(at, 2)
        return pltpu.make_async_copy(
            value_ref.at[plane_of(at)], raw.at[slot], load_sem.at[slot]
        )

    load(0).start()

    def device(place):
        return {"row": place // col_count, "col": lax.rem(place, col_count)}

    barrier = pltpu.get_barrier_semaphore()

    @pl.loop(1, devices)
    def _(step):
        pl.semaphore_signal(barrier, inc=1, device_id=device(lax.rem(me + step, devices)))

    pl.semaphore_wait(barrier, devices - 1)

    def swap(turn):
        return pltpu.make_async_remote_copy(
            src_ref=tiles.at[turn, :, :, 1 - core],
            dst_ref=mirror,
            send_sem=swap_sem.at[turn, 0],
            recv_sem=swap_sem.at[turn, 1],
            device_id=twin,
        )

    def trade(turn):
        return pltpu.make_async_remote_copy(
            src_ref=part.at[1],
            dst_ref=other,
            send_sem=swap_sem.at[turn, 2],
            recv_sem=swap_sem.at[turn, 3],
            device_id=twin,
        )

    def in_copy(turn, target, source):
        to_row = target // col_count
        to_col = lax.rem(target, col_count)
        from_row = source // col_count
        from_col = lax.rem(source, col_count)
        plane = turn * lot + to_row * deep + lax.rem(to_col // CORES, deep)
        return pltpu.make_async_remote_copy(
            src_ref=codes.at[plane, lax.rem(to_col, CORES)],
            dst_ref=tiles.at[turn, from_row, from_col // CORES, lax.rem(from_col, CORES)],
            send_sem=in_send.at[turn, target],
            recv_sem=in_recv.at[turn, source],
            device_id=device(target),
        )

    def inside(turn):
        return pltpu.make_async_copy(
            codes.at[turn * lot + mine, core],
            tiles.at[turn, row, col // CORES, core],
            load_sem.at[2 + turn],
        )

    def target_of(plane, half, side):
        spot = lax.rem(plane, lot)
        to_col = (half * deep + lax.rem(spot, deep)) * CORES + side
        return spot // deep * col_count + to_col

    @pl.loop(0, 2 * lot)
    def _(at):
        turn = at // lot

        @pl.when(at + 1 < 2 * lot)
        def _():
            load(at + 1).start()

        load(at).wait()
        plane = plane_of(at)
        codes[plane] = encode(raw[lax.rem(at, 2)]).reshape(codes.shape[1:])

        @pl.when(turn == 0)
        def _():
            for side in range(CORES):
                in_copy(0, target_of(plane, 1 - half_at, side), me).start()

        for side in range(CORES):
            target = target_of(plane, half_at, side)

            @pl.when(target != me)
            def _():
                in_copy(turn, target, me).start()

    for turn in range(2):
        inside(turn).start()

    build_tables(
        freq, time, flip_ref, pick_ref, size, lead_refs, minor_refs, half_at, deep, core
    )

    width = 2 * size
    piece = width // RADIX
    pairs = row_count // 2
    rows = lax.broadcasted_iota(jnp.int32, (size, width), 0)
    cols = lax.broadcasted_iota(jnp.int32, (size, width), 1)
    row_off = (rows + SP // 2) % SP - SP // 2
    col_off = (cols + SP // 2) % SP - SP // 2
    distance = (row_off * row_off + col_off * col_off).astype(jnp.float32)

    node_rows = lax.broadcasted_iota(jnp.int32, (size, bar_ref.shape[-1]), 0)
    node_cols = lax.broadcasted_iota(jnp.int32, (size, bar_ref.shape[-1]), 1)

    def build_masks(turn):
        @pl.loop(0, col_count)
        def _(tile):
            nodes = (node_rows + (tile * size + SP // 2)) // SP == node_cols
            nodes = nodes.astype(jnp.float32).astype(jnp.bfloat16)
            near, far = (
                dot32(nodes, bar_ref[turn, kind]).astype(jnp.bfloat16) for kind in range(2)
            )
            for pair in range(pairs):
                spot = pl.ds(pair * width, width)
                both = keep_scale(near, far, pick_ref[:, spot], distance)
                for kind in range(2):
                    mask[kind, tile, :, spot] = both[kind].astype(mask.dtype)

    build_masks(0)

    def take(turn):
        @pl.loop(1, devices)
        def _(step):
            in_copy(turn, me, lax.rem(me + step, devices)).wait_recv()

        inside(turn).wait()
        swap(turn).start()

    take(0)

    @pl.loop(0, lot)
    def _(at):
        plane = plane_of(lot + at)
        for side in range(CORES):
            in_copy(1, target_of(plane, 1 - half_at, side), me).start()

    def blend(turn, block, parity, reflected):
        tile = CORES * block + parity
        run = size // RADIX
        offset = pl.multiple_of(parity * run, run)
        for pair in range(pairs):
            spot = pl.ds(pair * width, width)
            turned = jnp.concatenate(
                [decode(tiles[turn, 2 * pair + up, block, parity]).T for up in range(2)], axis=1
            )
            across = jnp.concatenate(
                [decode(reflected(block, 2 * pair + up)) for up in range(2)], axis=1
            )
            by_mirror, by_direct = (
                mask[kind, tile, :, spot].astype(jnp.float32) for kind in range(2)
            )
            total = by_mirror * across + by_direct * turned
            lanes = mixed.shape[-1]
            strips = width // lanes
            for strip in range(strips):
                mixed[pair * strips + strip] = total[:, strip * lanes : (strip + 1) * lanes]
            for lead in range(RADIX):
                at = lead * row_count + block
                values = jnp.concatenate(
                    [
                        mixed[pair * strips + strip, pl.ds(lead, run, stride=RADIX), :]
                        for strip in range(strips)
                    ],
                    axis=1,
                )
                part[
                    at // (2 * RADIX), at // 2 % RADIX, at % 2, pl.ds(offset, run), spot
                ] = values.astype(part.dtype)

    def sort_columns():
        for lead in range(RADIX):
            start = lead * row_count // 2
            natural = part[start // RADIX, start % RADIX : start % RADIX + row_count // 2]
            natural = natural.reshape(-1, pairs * width)
            for pair in range(pairs):
                ready = dot32(natural[:, pair * width : (pair + 1) * width], flip_ref[...])
                ready = ready.astype(sym.dtype)
                for other_lead in range(RADIX):
                    spot = (other_lead * pairs + pair) * piece
                    sym[lead, :, spot : spot + piece] = ready[
                        :, other_lead * piece : (other_lead + 1) * piece
                    ]

    def blend_all(turn):
        @pl.loop(0, row_count)
        def _(block):
            blend(turn, block, core, lambda at, up: tiles[turn, at, up, core])

        swap(turn).wait()

        @pl.loop(0, row_count)
        def _(block):
            blend(turn, block, 1 - core, lambda at, up: mirror[at, up])

        sort_columns()

    count = part.shape[3]

    def first_all(turn):
        for side in (1, 0):
            res, ims = [], []
            for lead in range(RADIX):
                data = sym[lead]
                high = freq[0, lead, side].reshape(2 * count, -1)
                low = freq[1, lead, side].reshape(2 * count, -1)
                both = dot32(high, data) + dot32(low, data)
                res.append(both[:count])
                ims.append(both[count:])
            out_re, out_im = butterfly(res, ims)
            for block in range(RADIX):
                part[side, block, 0] = out_re[block].astype(part.dtype)
                part[side, block, 1] = out_im[block].astype(part.dtype)
            if side:
                trade(turn).start()

    def out_copy(turn, step, shift):
        to_row = lax.rem(row + step, row_count)
        to_layer = lax.rem(layer + shift, deep)
        return pltpu.make_async_remote_copy(
            src_ref=stage.at[to_row, to_layer],
            dst_ref=got_ref.at[turn, mine],
            send_sem=out_send.at[turn, step * deep + shift],
            recv_sem=out_recv.at[turn, step * deep + shift],
            device_id={"row": to_row, "col": base + CORES * to_layer + core},
        )

    def own(turn):
        return pltpu.make_async_copy(
            stage.at[row, layer], got_ref.at[turn, mine], out_recv.at[turn, 0]
        )

    half = part.shape[-1] // RADIX

    def second_all(turn):
        @pl.loop(0, row_count)
        def _(tick):
            step = lax.rem(tick + 1, row_count)
            block = lax.rem(row + step, row_count)
            res, ims = [], []
            for lead in range(RADIX):
                data = jnp.concatenate(
                    [
                        jnp.concatenate(
                            [
                                part[0, block, kind, :, lead * half : (lead + 1) * half],
                                other[block, kind, :, lead * half : (lead + 1) * half],
                            ],
                            axis=1,
                        )
                        for kind in range(2)
                    ],
                    axis=0,
                )
                broad = data.shape[1]
                both = dot32(data, time[lead, :broad]) + dot32(data, time[lead, broad:])
                res.append(both[:count, :broad] - both[count:, broad:])
                ims.append(both[:count, broad:] + both[count:, :broad])
            out_re, out_im = butterfly(res, ims)
            for kind, values in ((0, out_re), (1, out_im)):
                for quarter in range(RADIX):
                    ready = (values[quarter] * scale).astype(stage.dtype)
                    for at in range(deep):
                        stage[block, at, kind, :, quarter * broad : (quarter + 1) * broad] = (
                            ready[at * span : (at + 1) * span]
                        )
            for shift in range(1, deep):
                out_copy(turn, step, shift).start()

            @pl.when(step != 0)
            def _():
                out_copy(turn, step, 0).start()

            @pl.when(step == 0)
            def _():
                own(turn).start()

    blend_all(0)
    first_all(0)
    trade(0).wait()
    second_all(0)
    build_masks(1)
    take(1)
    blend_all(1)
    first_all(1)
    trade(1).wait()
    for at in range(1, lot):
        out_copy(0, at // deep, at % deep).wait_send()
    own(0).wait()
    second_all(1)
    own(1).wait()
    for turn in range(2):
        for at in range(1, lot):
            out_copy(turn, at // deep, at % deep).wait_recv()
    for at in range(1, lot):
        out_copy(1, at // deep, at % deep).wait_send()

    for turn in range(2):

        @pl.loop(1, devices)
        def _(step):
            in_copy(turn, lax.rem(me + step, devices), me).wait_send()


def angles(first_ids, second_ids, period):
    turns = np.mod(np.multiply.outer(first_ids, second_ids), period) * (2.0 * np.pi / period)
    return np.cos(turns).astype(np.float32), np.sin(turns).astype(np.float32)


def work(intensity, bars, scale, row_count, col_count):
    planes, h_block, size = intensity.shape
    devices = row_count * col_count
    deep = col_count // (HALVES * CORES)
    lot = row_count * deep
    length = row_count * h_block
    broad = length // RADIX
    width = row_count * size
    span = length // devices
    rows = deep * span
    bf16 = jnp.bfloat16
    fine = 16
    lead_ids = np.arange(RADIX)
    fine_ids = np.arange(fine)
    samples = RADIX * np.arange(broad)[None, :] + lead_ids[:, None]
    minor = np.arange(broad)
    coarse = [part[:, :, None] for part in angles(fine * np.arange(broad // fine), samples, length)]
    low = [part.transpose(1, 0, 2) for part in angles(fine_ids, samples, length)]
    base = [
        part[:, None] for part in angles(RADIX * fine * np.arange(broad // fine), minor, length)
    ]
    step = angles(RADIX * fine_ids[None, :] + lead_ids[:, None], minor, length)
    small = [jnp.asarray(part) for part in [*coarse, *low, *base, *step]]
    tile_shape = (row_count, col_count // CORES, CORES, size, size)
    return pl.pallas_call(
        lambda *refs: plane_kernel(scale, *refs),
        out_shape=jax.ShapeDtypeStruct((2, lot, 2, span, length), bf16),
        in_specs=[pl.BlockSpec(memory_space=pl.ANY)]
        + [pl.BlockSpec(memory_space=pltpu.VMEM)] * (1 + len(small)),
        out_specs=pl.BlockSpec(memory_space=pl.ANY),
        scratch_shapes=[
            pltpu.VMEM((2, h_block, size), jnp.float32),
            pltpu.VMEM((planes, CORES, size, size), jnp.int16),
            pltpu.VMEM((2,) + tile_shape, jnp.int16),
            pltpu.VMEM((row_count, row_count, size, size), jnp.int16),
            pltpu.VMEM((RADIX, broad, width), bf16),
            pltpu.VMEM((2, RADIX, CORES, 2, rows, broad), bf16),
            pltpu.VMEM((RADIX, 2 * broad, 2 * broad), bf16),
            pltpu.VMEM((CORES, RADIX, 2, rows, width), bf16),
            pltpu.VMEM((RADIX, 2, rows, width), bf16),
            pltpu.VMEM((RADIX, deep, 2, span, length), bf16),
            pltpu.VMEM((bars.shape[-1], width), bf16),
            pltpu.VMEM((2, col_count, size, width), bf16),
            pltpu.VMEM((2 * size, 2 * size), bf16),
            pltpu.VMEM((width // 128, size, 128), jnp.float32),
            pltpu.SemaphoreType.DMA((4,)),
            pltpu.SemaphoreType.DMA((2, devices)),
            pltpu.SemaphoreType.DMA((2, devices)),
            pltpu.SemaphoreType.DMA((2, 4)),
            pltpu.SemaphoreType.DMA((2, lot)),
            pltpu.SemaphoreType.DMA((2, lot)),
        ],
        compiler_params=pltpu.CompilerParams(
            collective_id=0, has_side_effects=True, vmem_limit_bytes=LIMIT
        ),
        cost_estimate=pl.CostEstimate(
            flops=140 * 10**9, bytes_accessed=10**7, transcendentals=0
        ),
    )(intensity, bars, *small)


def widen_kernel(got_ref, re_ref, im_ref, narrow, wide, in_sem, out_sem):
    count, slots = got_ref.shape[0], narrow.shape[0]

    def load(at):
        return pltpu.make_async_copy(got_ref.at[at], narrow.at[at % slots], in_sem.at[at % slots])

    def stores(at):
        return [
            pltpu.make_async_copy(
                wide.at[at % slots, kind], ref.at[at], out_sem.at[at % slots, kind]
            )
            for kind, ref in ((0, re_ref), (1, im_ref))
        ]

    for at in range(min(slots, count)):
        load(at).start()
    for at in range(count):
        load(at).wait()
        if at >= slots:
            for store in stores(at - slots):
                store.wait()
        for kind in range(2):
            wide[at % slots, kind] = narrow[at % slots, kind].astype(jnp.float32)
        for store in stores(at):
            store.start()
        if at + slots < count:
            load(at + slots).start()
    for at in range(max(count - slots, 0), count):
        for store in stores(at):
            store.wait()


def widen(got):
    count, _, span, length = got.shape
    slots = 8
    shape = jax.ShapeDtypeStruct((count, span, length), jnp.float32)
    return pl.pallas_call(
        widen_kernel,
        out_shape=(shape, shape),
        in_specs=[pl.BlockSpec(memory_space=pl.ANY)],
        out_specs=(pl.BlockSpec(memory_space=pl.ANY),) * 2,
        scratch_shapes=[
            pltpu.VMEM((slots, 2, span, length), got.dtype),
            pltpu.VMEM((slots, 2, span, length), jnp.float32),
            pltpu.SemaphoreType.DMA((slots,)),
            pltpu.SemaphoreType.DMA((slots, 2)),
        ],
        compiler_params=pltpu.CompilerParams(vmem_limit_bytes=LIMIT),
    )(got)


def plane_body(intensity, punch_radius):
    row_count = lax.axis_size("row")
    col_count = lax.axis_size("col")
    deep = col_count // (HALVES * CORES)
    planes, h_block, size = intensity.shape
    spot = lax.axis_index("row") * deep + lax.axis_index("col") // CORES % deep
    level = row_count * deep * jnp.arange(2, dtype=jnp.int32) + spot
    node = (level + SP // 2) // SP
    off = level - SP * node
    ids = jnp.arange(punch_radius.shape[0], dtype=jnp.int32)
    chosen = (node[:, None] == ids[None, :]).astype(jnp.int32)
    table = jnp.sum(chosen[:, :, None, None] * punch_radius[None], axis=1)
    table = (table - (off * off)[:, None, None]).astype(jnp.bfloat16)
    room = -table.shape[-1] % 256
    table = jnp.pad(table, ((0, 0), (0, room), (0, room)))
    bars = jnp.stack([table, jnp.swapaxes(table, 1, 2)], axis=1)
    got = work(intensity, bars, 1.0 / (h_block * row_count), row_count, col_count)
    return tuple(widen(got.reshape((planes,) + got.shape[2:])))


def body(intensity, punch_radius):
    row_count = lax.axis_size("row")
    col_count = lax.axis_size("col")
    planes, _, k_block = intensity.shape
    by_plane = row_count == RADIX and col_count == HALVES * RADIX
    by_plane = by_plane and 2 * planes == row_count * col_count and k_block % 256 == 0
    return (plane_body if by_plane else pencil_body)(intensity, punch_radius)


def solution(mesh):
    in_specs = (P(None, "row", "col"), P())
    out_specs = (P(None, ("row", "col"), None), P(None, ("row", "col"), None))
    return jax.shard_map(body, mesh=mesh, in_specs=in_specs, out_specs=out_specs, check_vma=False)
```

```python
import math

import jax
import jax.numpy as jnp
import numpy as np
from jax import lax
from jax.experimental import pallas as pl
from jax.experimental.pallas import tpu as pltpu
from jax.sharding import PartitionSpec as P

N = 2048
SP = 16


def circle(count, period, width):
    first_ids = jnp.arange(count, dtype=jnp.int32)
    second_ids = jnp.arange(width, dtype=jnp.int32)
    phases = first_ids[:, None] * second_ids[None, :] % period
    angles = phases.astype(jnp.float32) * (2.0 * math.pi / period)
    return (jnp.cos(angles), jnp.sin(angles))


def mixed(form, left, right):
    return jnp.einsum(form, left, right, precision=lax.Precision.HIGHEST)


def spectral(real_in, imag_in):
    length = real_in.shape[-1]
    first = 32
    second = length // first
    shape_lead = real_in.shape[:-1]
    cos_first, sin_first = circle(first, first, first)
    cos_twist, sin_twist = circle(first, length, second)
    cos_second, sin_second = circle(second, second, second)
    grid_re = real_in.reshape(shape_lead + (first, second))
    section_re = mixed("...ab,ac->...cb", grid_re, cos_first)
    section_im = mixed("...ab,ac->...cb", grid_re, sin_first)
    grid_im = imag_in.reshape(shape_lead + (first, second))
    section_re = section_re - mixed("...ab,ac->...cb", grid_im, sin_first)
    section_im = section_im + mixed("...ab,ac->...cb", grid_im, cos_first)
    twist_re = section_re * cos_twist - section_im * sin_twist
    twist_im = section_re * sin_twist + section_im * cos_twist
    final_re = mixed("...cb,bd->...dc", twist_re, cos_second) - mixed(
        "...cb,bd->...dc", twist_im, sin_second
    )
    final_im = mixed("...cb,bd->...dc", twist_re, sin_second) + mixed(
        "...cb,bd->...dc", twist_im, cos_second
    )
    return (final_re.reshape(shape_lead + (length,)), final_im.reshape(shape_lead + (length,)))


def spectral_lead(real_in):
    row_total, length = real_in.shape
    first = 32
    second = length // first
    cos_first, sin_first = circle(first, first, first)
    cos_twist, sin_twist = circle(first, length, second)
    cos_second, sin_second = circle(second, second, second)
    grid_re = real_in.reshape(row_total, first, second)
    section_re = mixed("rab,ac->cbr", grid_re, cos_first)
    section_im = mixed("rab,ac->cbr", grid_re, sin_first)
    twist_re = section_re * cos_twist[:, :, None] - section_im * sin_twist[:, :, None]
    twist_im = section_re * sin_twist[:, :, None] + section_im * cos_twist[:, :, None]
    final_re = mixed("cbr,bd->dcr", twist_re, cos_second) - mixed(
        "cbr,bd->dcr", twist_im, sin_second
    )
    final_im = mixed("cbr,bd->dcr", twist_re, sin_second) + mixed(
        "cbr,bd->dcr", twist_im, cos_second
    )
    return (final_re.reshape(length, row_total), final_im.reshape(length, row_total))


def keep_map(first_coords, second_coords, radius_table, levels):
    node_count = radius_table.shape[1]
    first_node = (first_coords + SP // 2) // SP
    first_dist = first_coords - SP * first_node
    second_node = (second_coords + SP // 2) // SP
    second_dist = second_coords - SP * second_node
    plane_node = (levels + SP // 2) // SP
    plane_dist = levels - SP * plane_node
    node_ids = jnp.arange(node_count, dtype=jnp.int32)
    pick_first = (first_node[:, None] == node_ids[None, :]).astype(jnp.bfloat16)
    pick_second = (second_node[:, None] == node_ids[None, :]).astype(jnp.bfloat16)
    table_half = jnp.einsum(
        "hn,snm->shm",
        pick_first,
        radius_table.astype(jnp.bfloat16),
        preferred_element_type=jnp.float32,
    ).astype(jnp.bfloat16)
    plane_radius = jnp.einsum(
        "shm,km->shk", table_half, pick_second, preferred_element_type=jnp.float32
    )
    level_ids = jnp.arange(radius_table.shape[0], dtype=jnp.int32)
    pick_plane = (plane_node[:, None] == level_ids[None, :]).astype(jnp.float32)
    radius = jnp.einsum("ls,shk->hlk", pick_plane, plane_radius, precision=lax.Precision.HIGHEST)
    distance = (
        (first_dist * first_dist)[:, None, None]
        + (plane_dist * plane_dist)[None, :, None]
        + (second_dist * second_dist)[None, None, :]
    )
    return (distance.astype(jnp.float32) >= radius).astype(jnp.float32)


def pencil_body(intensity, punch_radius):
    row_count = lax.axis_size("row")
    col_count = lax.axis_size("col")
    row_at = lax.axis_index("row")
    col_at = lax.axis_index("col")
    planes, h_block, k_block = intensity.shape
    groups = col_count // row_count
    fine_width = k_block // col_count
    pencil_rows = groups * fine_width
    levels = jnp.arange(planes, dtype=jnp.int32)
    swapped_table = jnp.swapaxes(punch_radius, 1, 2)
    outgoing = jnp.transpose(
        intensity.reshape(planes, h_block, col_count, fine_width), (2, 3, 0, 1)
    )
    arrived = lax.all_to_all(
        lax.all_to_all(outgoing, "col", split_axis=0, concat_axis=0, tiled=True),
        "row",
        split_axis=0,
        concat_axis=3,
        tiled=True,
    )
    pencil_h = (
        h_block * row_at
        + k_block * jnp.arange(groups, dtype=jnp.int32)[:, None]
        + fine_width * col_at
        + jnp.arange(fine_width, dtype=jnp.int32)[None, :]
    ).reshape(-1)
    whole_k = jnp.arange(N, dtype=jnp.int32)
    mirrored = arrived.reshape(pencil_rows, planes, N)
    pencil_input = jnp.transpose(
        intensity.reshape(planes, groups, col_count, fine_width, k_block), (1, 2, 3, 0, 4)
    )
    direct = lax.all_to_all(pencil_input, "col", split_axis=1, concat_axis=4, tiled=True).reshape(
        pencil_rows, planes, N
    )
    keep_mask = keep_map(pencil_h, whole_k, punch_radius, levels)
    keep_swap = keep_map(pencil_h, whole_k, swapped_table, levels)
    counts = jnp.maximum(keep_mask + keep_swap, 1.0)
    symmetric = ((keep_mask * direct + keep_swap * mirrored) / counts).astype(jnp.bfloat16)
    row_total = pencil_rows * planes
    flat_rows = symmetric.reshape(row_total, N).astype(jnp.float32)
    part_re, part_im = spectral_lead(flat_rows)
    freq_width = N // (row_count * col_count)
    sectioned = jnp.stack([part_re, part_im]).reshape(
        2, row_count, col_count, freq_width, row_total
    )
    spectra = lax.all_to_all(
        lax.all_to_all(sectioned, "row", split_axis=1, concat_axis=1, tiled=True),
        "col",
        split_axis=2,
        concat_axis=2,
        tiled=True,
    )
    spectra = spectra.reshape(2, row_count, col_count, freq_width, groups, fine_width, planes)
    spectra = jnp.transpose(spectra, (0, 6, 3, 1, 4, 2, 5)).reshape(2, planes * freq_width, N)
    final_re, final_im = spectral(spectra[0], spectra[1])
    out_re = (final_re / N).reshape(planes, freq_width, N)
    out_im = (final_im / N).reshape(planes, freq_width, N)
    return (out_re, out_im)


RADIX = 4
HALVES = 2
CORES = 2
CURVE = 7
CODE_BITS = 102
UNIT = 2.0**-CODE_BITS
LIMIT = 60 * 1024 * 1024


def dot32(left, right):
    return jnp.dot(left, right, preferred_element_type=jnp.float32)


def butterfly(res, ims):
    even_re, odd_re = res[0] + res[2], res[0] - res[2]
    even_im, odd_im = ims[0] + ims[2], ims[0] - ims[2]
    pair_re, gap_re = res[1] + res[3], res[1] - res[3]
    pair_im, gap_im = ims[1] + ims[3], ims[1] - ims[3]
    out_re = (even_re + pair_re, odd_re - gap_im, even_re - pair_re, odd_re + gap_im)
    out_im = (even_im + pair_im, odd_im + gap_re, even_im - pair_im, odd_im - gap_re)
    return out_re, out_im


def encode(values):
    size = jnp.exp2(jnp.log2(jnp.abs(values)) * (1.0 / CURVE)) * 2.0 ** (CODE_BITS / CURVE)
    return jnp.where(values < 0, -jnp.round(size), jnp.round(size)).astype(jnp.int32).astype(jnp.int16)


def decode(codes):
    base = codes.astype(jnp.int32).astype(jnp.float32)
    square = base * base
    return (square * square) * (square * base)


def keep_scale(near, far, picked, distance):
    keep_mirror = distance >= dot32(near, picked)
    keep_direct = distance >= dot32(far, picked)
    scale = jnp.where(keep_mirror & keep_direct, 0.5 * UNIT, UNIT)
    return jnp.where(keep_mirror, scale, 0.0), jnp.where(keep_direct, scale, 0.0)


def build_tables(freq, time, flip, pick, size, lead_refs, minor_refs, half, layer_count, core):
    coarse_re, coarse_im, fine_re, fine_im = lead_refs
    fine = fine_re.shape[1]
    _, _, _, _, rows, width = freq.shape
    runs = rows // fine
    inner = runs // layer_count

    @pl.loop(0, RADIX * CORES * runs)
    def _(at):
        lead, rest = at // (CORES * runs), lax.rem(at, CORES * runs)
        side, run = rest // runs, lax.rem(rest, runs)
        owner = core + side * (1 - 2 * core)
        start = (half * layer_count + run // inner) * CORES * inner
        start = start + owner * inner + lax.rem(run, inner)
        big_re, big_im = coarse_re[start, lead], coarse_im[start, lead]
        low_re, low_im = fine_re[lead], fine_im[lead]
        place = pl.ds(pl.multiple_of(run * fine, fine), fine)
        for kind, full in (
            (0, big_re * low_re - big_im * low_im),
            (1, big_re * low_im + big_im * low_re),
        ):
            high = full.astype(jnp.bfloat16)
            freq[0, lead, side, kind, place] = high
            freq[1, lead, side, kind, place] = (full - high.astype(jnp.float32)).astype(
                jnp.bfloat16
            )

    base_re, base_im, step_re, step_im = minor_refs
    blocks = width // fine
    tile_runs = blocks // (CORES * RADIX)

    @pl.loop(0, RADIX * blocks)
    def _(at):
        lead, run = at // blocks, lax.rem(at, blocks)
        rel, rest = run // (blocks // CORES), lax.rem(run, blocks // CORES)
        owner = core + rel * (1 - 2 * core)
        start = (CORES * (rest // tile_runs) + owner) * tile_runs + lax.rem(rest, tile_runs)
        big_re, big_im = base_re[start], base_im[start]
        low_re, low_im = step_re[lead], step_im[lead]
        for kind, full in (
            (0, big_re * low_re - big_im * low_im),
            (1, big_re * low_im + big_im * low_re),
        ):
            high = full.astype(jnp.bfloat16)
            low = (full - high.astype(jnp.float32)).astype(jnp.bfloat16)
            for level, values in ((0, high), (1, low)):
                place = pl.ds(pl.multiple_of(level * width + run * fine, fine), fine)
                time[lead, place, kind * width : (kind + 1) * width] = values

    wide = flip.shape[0]
    piece = size // RADIX
    rows = lax.broadcasted_iota(jnp.int32, (wide, wide), 0)
    cols = lax.broadcasted_iota(jnp.int32, (wide, wide), 1)
    source = cols // piece % 2 * size + RADIX * (cols % piece) + cols // (2 * piece)
    flip[...] = (source == rows).astype(jnp.float32).astype(jnp.bfloat16)
    rows = lax.broadcasted_iota(jnp.int32, pick.shape, 0)
    cols = lax.broadcasted_iota(jnp.int32, pick.shape, 1)
    coord = (cols // size * CORES + core) * size + cols % size
    pick[...] = ((coord + SP // 2) // SP == rows).astype(jnp.float32).astype(jnp.bfloat16)


def plane_kernel(scale, value_ref, bar_ref, *refs):
    lead_refs, minor_refs, refs = refs[:4], refs[4:8], refs[8:]
    got_ref, raw, codes, tiles, mirror, sym, freq, time, part, other, stage = refs[:11]
    pick_ref, mask, flip_ref, mixed = refs[11:15]
    load_sem, in_send, in_recv, swap_sem, out_send, out_recv = refs[15:]
    row_count = lax.axis_size("row")
    col_count = lax.axis_size("col")
    row = lax.axis_index("row")
    col = lax.axis_index("col")
    core = lax.rem(col, CORES)
    deep, span = stage.shape[1], stage.shape[3]
    size = tiles.shape[-1]
    layer = lax.rem(col // CORES, deep)
    base = col - core - CORES * layer
    half_at = col // (CORES * deep)
    mine = row * deep + layer
    lot = row_count * deep
    me = row * col_count + col
    devices = row_count * col_count
    twin = {"col": col + 1 - 2 * core}

    def plane_of(at):
        step = lax.rem(at, lot)
        step = core * (lot - 1 - step) + (1 - core) * step
        high, low = row // 2 + step // deep // 2, lax.rem(row, 2) + lax.rem(step // deep, 2)
        to_row = lax.rem(high, row_count // 2) * 2 + lax.rem(low, 2)
        return at // lot * lot + to_row * deep + lax.rem(layer + step, deep)

    def load(at):
        slot = lax.rem(at, 2)
        return pltpu.make_async_copy(
            value_ref.at[plane_of(at)], raw.at[slot], load_sem.at[slot]
        )

    load(0).start()

    def device(place):
        return {"row": place // col_count, "col": lax.rem(place, col_count)}

    barrier = pltpu.get_barrier_semaphore()

    @pl.loop(1, devices)
    def _(step):
        pl.semaphore_signal(barrier, inc=1, device_id=device(lax.rem(me + step, devices)))

    pl.semaphore_wait(barrier, devices - 1)

    def swap(turn):
        return pltpu.make_async_remote_copy(
            src_ref=tiles.at[turn, :, :, 1 - core],
            dst_ref=mirror,
            send_sem=swap_sem.at[turn, 0],
            recv_sem=swap_sem.at[turn, 1],
            device_id=twin,
        )

    def trade(turn):
        return pltpu.make_async_remote_copy(
            src_ref=part.at[1],
            dst_ref=other,
            send_sem=swap_sem.at[turn, 2],
            recv_sem=swap_sem.at[turn, 3],
            device_id=twin,
        )

    def in_copy(turn, target, source):
        to_row = target // col_count
        to_col = lax.rem(target, col_count)
        from_row = source // col_count
        from_col = lax.rem(source, col_count)
        plane = turn * lot + to_row * deep + lax.rem(to_col // CORES, deep)
        return pltpu.make_async_remote_copy(
            src_ref=codes.at[plane, lax.rem(to_col, CORES)],
            dst_ref=tiles.at[turn, from_row, from_col // CORES, lax.rem(from_col, CORES)],
            send_sem=in_send.at[turn, target],
            recv_sem=in_recv.at[turn, source],
            device_id=device(target),
        )

    def inside(turn):
        return pltpu.make_async_copy(
            codes.at[turn * lot + mine, core],
            tiles.at[turn, row, col // CORES, core],
            load_sem.at[2 + turn],
        )

    def target_of(plane, half, side):
        spot = lax.rem(plane, lot)
        to_col = (half * deep + lax.rem(spot, deep)) * CORES + side
        return spot // deep * col_count + to_col

    @pl.loop(0, 2 * lot)
    def _(at):
        turn = at // lot

        @pl.when(at + 1 < 2 * lot)
        def _():
            load(at + 1).start()

        load(at).wait()
        plane = plane_of(at)
        codes[plane] = encode(raw[lax.rem(at, 2)]).reshape(codes.shape[1:])

        @pl.when(turn == 0)
        def _():
            for side in range(CORES):
                in_copy(0, target_of(plane, 1 - half_at, side), me).start()

        for side in range(CORES):
            target = target_of(plane, half_at, side)

            @pl.when(target != me)
            def _():
                in_copy(turn, target, me).start()

    for turn in range(2):
        inside(turn).start()

    build_tables(
        freq, time, flip_ref, pick_ref, size, lead_refs, minor_refs, half_at, deep, core
    )

    width = 2 * size
    piece = width // RADIX
    pairs = row_count // 2
    rows = lax.broadcasted_iota(jnp.int32, (size, width), 0)
    cols = lax.broadcasted_iota(jnp.int32, (size, width), 1)
    row_off = (rows + SP // 2) % SP - SP // 2
    col_off = (cols + SP // 2) % SP - SP // 2
    distance = (row_off * row_off + col_off * col_off).astype(jnp.float32)

    node_rows = lax.broadcasted_iota(jnp.int32, (size, bar_ref.shape[-1]), 0)
    node_cols = lax.broadcasted_iota(jnp.int32, (size, bar_ref.shape[-1]), 1)

    def build_masks(turn):
        @pl.loop(0, col_count)
        def _(tile):
            nodes = (node_rows + (tile * size + SP // 2)) // SP == node_cols
            nodes = nodes.astype(jnp.float32).astype(jnp.bfloat16)
            near, far = (
                dot32(nodes, bar_ref[turn, kind]).astype(jnp.bfloat16) for kind in range(2)
            )
            for pair in range(pairs):
                spot = pl.ds(pair * width, width)
                both = keep_scale(near, far, pick_ref[:, spot], distance)
                for kind in range(2):
                    mask[kind, tile, :, spot] = both[kind].astype(mask.dtype)

    build_masks(0)

    def take(turn):
        @pl.loop(1, devices)
        def _(step):
            in_copy(turn, me, lax.rem(me + step, devices)).wait_recv()

        inside(turn).wait()
        swap(turn).start()

    take(0)

    @pl.loop(0, lot)
    def _(at):
        plane = plane_of(lot + at)
        for side in range(CORES):
            in_copy(1, target_of(plane, 1 - half_at, side), me).start()

    def blend(turn, block, parity, reflected):
        tile = CORES * block + parity
        run = size // RADIX
        offset = pl.multiple_of(parity * run, run)
        for pair in range(pairs):
            spot = pl.ds(pair * width, width)
            turned = jnp.concatenate(
                [decode(tiles[turn, 2 * pair + up, block, parity]).T for up in range(2)], axis=1
            )
            across = jnp.concatenate(
                [decode(reflected(block, 2 * pair + up)) for up in range(2)], axis=1
            )
            by_mirror, by_direct = (
                mask[kind, tile, :, spot].astype(jnp.float32) for kind in range(2)
            )
            total = by_mirror * across + by_direct * turned
            lanes = mixed.shape[-1]
            strips = width // lanes
            for strip in range(strips):
                mixed[pair * strips + strip] = total[:, strip * lanes : (strip + 1) * lanes]
            for lead in range(RADIX):
                at = lead * row_count + block
                values = jnp.concatenate(
                    [
                        mixed[pair * strips + strip, pl.ds(lead, run, stride=RADIX), :]
                        for strip in range(strips)
                    ],
                    axis=1,
                )
                part[
                    at // (2 * RADIX), at // 2 % RADIX, at % 2, pl.ds(offset, run), spot
                ] = values.astype(part.dtype)

    def sort_columns():
        for lead in range(RADIX):
            start = lead * row_count // 2
            natural = part[start // RADIX, start % RADIX : start % RADIX + row_count // 2]
            natural = natural.reshape(-1, pairs * width)
            for pair in range(pairs):
                ready = dot32(natural[:, pair * width : (pair + 1) * width], flip_ref[...])
                ready = ready.astype(sym.dtype)
                for other_lead in range(RADIX):
                    spot = (other_lead * pairs + pair) * piece
                    sym[lead, :, spot : spot + piece] = ready[
                        :, other_lead * piece : (other_lead + 1) * piece
                    ]

    def blend_all(turn):
        @pl.loop(0, row_count)
        def _(block):
            blend(turn, block, core, lambda at, up: tiles[turn, at, up, core])

        swap(turn).wait()

        @pl.loop(0, row_count)
        def _(block):
            blend(turn, block, 1 - core, lambda at, up: mirror[at, up])

        sort_columns()

    count = part.shape[3]

    def first_all(turn):
        for side in (1, 0):
            res, ims = [], []
            for lead in range(RADIX):
                data = sym[lead]
                high = freq[0, lead, side].reshape(2 * count, -1)
                low = freq[1, lead, side].reshape(2 * count, -1)
                both = dot32(high, data) + dot32(low, data)
                res.append(both[:count])
                ims.append(both[count:])
            out_re, out_im = butterfly(res, ims)
            for block in range(RADIX):
                part[side, block, 0] = out_re[block].astype(part.dtype)
                part[side, block, 1] = out_im[block].astype(part.dtype)
            if side:
                trade(turn).start()

    def partner(step):
        high, low = row // 2 + step // 2, lax.rem(row, 2) + lax.rem(step, 2)
        return lax.rem(high, row_count // 2) * 2 + lax.rem(low, 2)

    def out_copy(turn, step, shift):
        to_row = partner(step)
        to_layer = lax.rem(layer + shift, deep)
        return pltpu.make_async_remote_copy(
            src_ref=stage.at[to_row, to_layer],
            dst_ref=got_ref.at[turn, mine],
            send_sem=out_send.at[turn, step * deep + shift],
            recv_sem=out_recv.at[turn, step * deep + shift],
            device_id={"row": to_row, "col": base + CORES * to_layer + core},
        )

    def own(turn):
        return pltpu.make_async_copy(
            stage.at[row, layer], got_ref.at[turn, mine], out_recv.at[turn, 0]
        )

    half = part.shape[-1] // RADIX

    def second_all(turn):
        @pl.loop(0, row_count)
        def _(tick):
            away = row_count - 1 - tick
            step = core * (lax.rem(tick, 2) * 2 + tick // 2)
            step = step + (1 - core) * (lax.rem(away, 2) * 2 + away // 2)
            block = partner(step)
            if turn:
                for shift in range(1, deep):
                    out_copy(0, step, shift).wait_send()

                @pl.when(step != 0)
                def _():
                    out_copy(0, step, 0).wait_send()

                @pl.when(step == 0)
                def _():
                    own(0).wait()

            res, ims = [], []
            for lead in range(RADIX):
                data = jnp.concatenate(
                    [
                        jnp.concatenate(
                            [
                                part[0, block, kind, :, lead * half : (lead + 1) * half],
                                other[block, kind, :, lead * half : (lead + 1) * half],
                            ],
                            axis=1,
                        )
                        for kind in range(2)
                    ],
                    axis=0,
                )
                broad = data.shape[1]
                both = dot32(data, time[lead, :broad]) + dot32(data, time[lead, broad:])
                res.append(both[:count, :broad] - both[count:, broad:])
                ims.append(both[:count, broad:] + both[count:, :broad])
            out_re, out_im = butterfly(res, ims)
            for kind, values in ((0, out_re), (1, out_im)):
                for quarter in range(RADIX):
                    ready = (values[quarter] * scale).astype(stage.dtype)
                    for at in range(deep):
                        stage[block, at, kind, :, quarter * broad : (quarter + 1) * broad] = (
                            ready[at * span : (at + 1) * span]
                        )
            for shift in range(1, deep):
                out_copy(turn, step, shift).start()

            @pl.when(step != 0)
            def _():
                out_copy(turn, step, 0).start()

            @pl.when(step == 0)
            def _():
                own(turn).start()

    blend_all(0)
    first_all(0)
    trade(0).wait()
    second_all(0)
    build_masks(1)
    take(1)
    blend_all(1)
    first_all(1)
    trade(1).wait()
    second_all(1)
    own(1).wait()
    for turn in range(2):
        for at in range(1, lot):
            out_copy(turn, at // deep, at % deep).wait_recv()
    for at in range(1, lot):
        out_copy(1, at // deep, at % deep).wait_send()

    for turn in range(2):

        @pl.loop(1, devices)
        def _(step):
            in_copy(turn, lax.rem(me + step, devices), me).wait_send()


def angles(first_ids, second_ids, period):
    turns = np.mod(np.multiply.outer(first_ids, second_ids), period) * (2.0 * np.pi / period)
    return np.cos(turns).astype(np.float32), np.sin(turns).astype(np.float32)


def work(intensity, bars, scale, row_count, col_count):
    planes, h_block, size = intensity.shape
    devices = row_count * col_count
    deep = col_count // (HALVES * CORES)
    lot = row_count * deep
    length = row_count * h_block
    broad = length // RADIX
    width = row_count * size
    span = length // devices
    rows = deep * span
    bf16 = jnp.bfloat16
    fine = 16
    lead_ids = np.arange(RADIX)
    fine_ids = np.arange(fine)
    samples = RADIX * np.arange(broad)[None, :] + lead_ids[:, None]
    minor = np.arange(broad)
    coarse = [part[:, :, None] for part in angles(fine * np.arange(broad // fine), samples, length)]
    low = [part.transpose(1, 0, 2) for part in angles(fine_ids, samples, length)]
    base = [
        part[:, None] for part in angles(RADIX * fine * np.arange(broad // fine), minor, length)
    ]
    step = angles(RADIX * fine_ids[None, :] + lead_ids[:, None], minor, length)
    small = [jnp.asarray(part) for part in [*coarse, *low, *base, *step]]
    tile_shape = (row_count, col_count // CORES, CORES, size, size)
    return pl.pallas_call(
        lambda *refs: plane_kernel(scale, *refs),
        out_shape=jax.ShapeDtypeStruct((2, lot, 2, span, length), bf16),
        in_specs=[pl.BlockSpec(memory_space=pl.ANY)]
        + [pl.BlockSpec(memory_space=pltpu.VMEM)] * (1 + len(small)),
        out_specs=pl.BlockSpec(memory_space=pl.ANY),
        scratch_shapes=[
            pltpu.VMEM((2, h_block, size), jnp.float32),
            pltpu.VMEM((planes, CORES, size, size), jnp.int16),
            pltpu.VMEM((2,) + tile_shape, jnp.int16),
            pltpu.VMEM((row_count, row_count, size, size), jnp.int16),
            pltpu.VMEM((RADIX, broad, width), bf16),
            pltpu.VMEM((2, RADIX, CORES, 2, rows, broad), bf16),
            pltpu.VMEM((RADIX, 2 * broad, 2 * broad), bf16),
            pltpu.VMEM((CORES, RADIX, 2, rows, width), bf16),
            pltpu.VMEM((RADIX, 2, rows, width), bf16),
            pltpu.VMEM((RADIX, deep, 2, span, length), bf16),
            pltpu.VMEM((bars.shape[-1], width), bf16),
            pltpu.VMEM((2, col_count, size, width), bf16),
            pltpu.VMEM((2 * size, 2 * size), bf16),
            pltpu.VMEM((width // 128, size, 128), jnp.float32),
            pltpu.SemaphoreType.DMA((4,)),
            pltpu.SemaphoreType.DMA((2, devices)),
            pltpu.SemaphoreType.DMA((2, devices)),
            pltpu.SemaphoreType.DMA((2, 4)),
            pltpu.SemaphoreType.DMA((2, lot)),
            pltpu.SemaphoreType.DMA((2, lot)),
        ],
        compiler_params=pltpu.CompilerParams(
            collective_id=0, has_side_effects=True, vmem_limit_bytes=LIMIT
        ),
        cost_estimate=pl.CostEstimate(
            flops=140 * 10**9, bytes_accessed=10**7, transcendentals=0
        ),
    )(intensity, bars, *small)


def widen_kernel(got_ref, re_ref, im_ref, narrow, wide, in_sem, out_sem):
    count, slots = got_ref.shape[0], narrow.shape[0]

    def load(at):
        return pltpu.make_async_copy(got_ref.at[at], narrow.at[at % slots], in_sem.at[at % slots])

    def stores(at):
        return [
            pltpu.make_async_copy(
                wide.at[at % slots, kind], ref.at[at], out_sem.at[at % slots, kind]
            )
            for kind, ref in ((0, re_ref), (1, im_ref))
        ]

    for at in range(min(slots, count)):
        load(at).start()
    for at in range(count):
        load(at).wait()
        if at >= slots:
            for store in stores(at - slots):
                store.wait()
        for kind in range(2):
            wide[at % slots, kind] = narrow[at % slots, kind].astype(jnp.float32)
        for store in stores(at):
            store.start()
        if at + slots < count:
            load(at + slots).start()
    for at in range(max(count - slots, 0), count):
        for store in stores(at):
            store.wait()


def widen(got):
    count, _, span, length = got.shape
    slots = 8
    shape = jax.ShapeDtypeStruct((count, span, length), jnp.float32)
    return pl.pallas_call(
        widen_kernel,
        out_shape=(shape, shape),
        in_specs=[pl.BlockSpec(memory_space=pl.ANY)],
        out_specs=(pl.BlockSpec(memory_space=pl.ANY),) * 2,
        scratch_shapes=[
            pltpu.VMEM((slots, 2, span, length), got.dtype),
            pltpu.VMEM((slots, 2, span, length), jnp.float32),
            pltpu.SemaphoreType.DMA((slots,)),
            pltpu.SemaphoreType.DMA((slots, 2)),
        ],
        compiler_params=pltpu.CompilerParams(vmem_limit_bytes=LIMIT),
    )(got)


def plane_body(intensity, punch_radius):
    row_count = lax.axis_size("row")
    col_count = lax.axis_size("col")
    deep = col_count // (HALVES * CORES)
    planes, h_block, size = intensity.shape
    spot = lax.axis_index("row") * deep + lax.axis_index("col") // CORES % deep
    level = row_count * deep * jnp.arange(2, dtype=jnp.int32) + spot
    node = (level + SP // 2) // SP
    off = level - SP * node
    ids = jnp.arange(punch_radius.shape[0], dtype=jnp.int32)
    chosen = (node[:, None] == ids[None, :]).astype(jnp.int32)
    table = jnp.sum(chosen[:, :, None, None] * punch_radius[None], axis=1)
    table = (table - (off * off)[:, None, None]).astype(jnp.bfloat16)
    room = -table.shape[-1] % 256
    table = jnp.pad(table, ((0, 0), (0, room), (0, room)))
    bars = jnp.stack([table, jnp.swapaxes(table, 1, 2)], axis=1)
    got = work(intensity, bars, 1.0 / (h_block * row_count), row_count, col_count)
    return tuple(widen(got.reshape((planes,) + got.shape[2:])))


def body(intensity, punch_radius):
    row_count = lax.axis_size("row")
    col_count = lax.axis_size("col")
    planes, _, k_block = intensity.shape
    by_plane = row_count == RADIX and col_count == HALVES * RADIX
    by_plane = by_plane and 2 * planes == row_count * col_count and k_block % 256 == 0
    return (plane_body if by_plane else pencil_body)(intensity, punch_radius)


def solution(mesh):
    in_specs = (P(None, "row", "col"), P())
    out_specs = (P(None, ("row", "col"), None), P(None, ("row", "col"), None))
    return jax.shard_map(body, mesh=mesh, in_specs=in_specs, out_specs=out_specs, check_vma=False)
```

```python
import math

import jax
import jax.numpy as jnp
import numpy as np
from jax import lax
from jax.experimental import pallas as pl
from jax.experimental.pallas import tpu as pltpu
from jax.sharding import PartitionSpec as P

N = 2048
SP = 16


def circle(count, period, width):
    first_ids = jnp.arange(count, dtype=jnp.int32)
    second_ids = jnp.arange(width, dtype=jnp.int32)
    phases = first_ids[:, None] * second_ids[None, :] % period
    angles = phases.astype(jnp.float32) * (2.0 * math.pi / period)
    return (jnp.cos(angles), jnp.sin(angles))


def mixed(form, left, right):
    return jnp.einsum(form, left, right, precision=lax.Precision.HIGHEST)


def spectral(real_in, imag_in):
    length = real_in.shape[-1]
    first = 32
    second = length // first
    shape_lead = real_in.shape[:-1]
    cos_first, sin_first = circle(first, first, first)
    cos_twist, sin_twist = circle(first, length, second)
    cos_second, sin_second = circle(second, second, second)
    grid_re = real_in.reshape(shape_lead + (first, second))
    section_re = mixed("...ab,ac->...cb", grid_re, cos_first)
    section_im = mixed("...ab,ac->...cb", grid_re, sin_first)
    grid_im = imag_in.reshape(shape_lead + (first, second))
    section_re = section_re - mixed("...ab,ac->...cb", grid_im, sin_first)
    section_im = section_im + mixed("...ab,ac->...cb", grid_im, cos_first)
    twist_re = section_re * cos_twist - section_im * sin_twist
    twist_im = section_re * sin_twist + section_im * cos_twist
    final_re = mixed("...cb,bd->...dc", twist_re, cos_second) - mixed(
        "...cb,bd->...dc", twist_im, sin_second
    )
    final_im = mixed("...cb,bd->...dc", twist_re, sin_second) + mixed(
        "...cb,bd->...dc", twist_im, cos_second
    )
    return (final_re.reshape(shape_lead + (length,)), final_im.reshape(shape_lead + (length,)))


def spectral_lead(real_in):
    row_total, length = real_in.shape
    first = 32
    second = length // first
    cos_first, sin_first = circle(first, first, first)
    cos_twist, sin_twist = circle(first, length, second)
    cos_second, sin_second = circle(second, second, second)
    grid_re = real_in.reshape(row_total, first, second)
    section_re = mixed("rab,ac->cbr", grid_re, cos_first)
    section_im = mixed("rab,ac->cbr", grid_re, sin_first)
    twist_re = section_re * cos_twist[:, :, None] - section_im * sin_twist[:, :, None]
    twist_im = section_re * sin_twist[:, :, None] + section_im * cos_twist[:, :, None]
    final_re = mixed("cbr,bd->dcr", twist_re, cos_second) - mixed(
        "cbr,bd->dcr", twist_im, sin_second
    )
    final_im = mixed("cbr,bd->dcr", twist_re, sin_second) + mixed(
        "cbr,bd->dcr", twist_im, cos_second
    )
    return (final_re.reshape(length, row_total), final_im.reshape(length, row_total))


def keep_map(first_coords, second_coords, radius_table, levels):
    node_count = radius_table.shape[1]
    first_node = (first_coords + SP // 2) // SP
    first_dist = first_coords - SP * first_node
    second_node = (second_coords + SP // 2) // SP
    second_dist = second_coords - SP * second_node
    plane_node = (levels + SP // 2) // SP
    plane_dist = levels - SP * plane_node
    node_ids = jnp.arange(node_count, dtype=jnp.int32)
    pick_first = (first_node[:, None] == node_ids[None, :]).astype(jnp.bfloat16)
    pick_second = (second_node[:, None] == node_ids[None, :]).astype(jnp.bfloat16)
    table_half = jnp.einsum(
        "hn,snm->shm",
        pick_first,
        radius_table.astype(jnp.bfloat16),
        preferred_element_type=jnp.float32,
    ).astype(jnp.bfloat16)
    plane_radius = jnp.einsum(
        "shm,km->shk", table_half, pick_second, preferred_element_type=jnp.float32
    )
    level_ids = jnp.arange(radius_table.shape[0], dtype=jnp.int32)
    pick_plane = (plane_node[:, None] == level_ids[None, :]).astype(jnp.float32)
    radius = jnp.einsum("ls,shk->hlk", pick_plane, plane_radius, precision=lax.Precision.HIGHEST)
    distance = (
        (first_dist * first_dist)[:, None, None]
        + (plane_dist * plane_dist)[None, :, None]
        + (second_dist * second_dist)[None, None, :]
    )
    return (distance.astype(jnp.float32) >= radius).astype(jnp.float32)


def pencil_body(intensity, punch_radius):
    row_count = lax.axis_size("row")
    col_count = lax.axis_size("col")
    row_at = lax.axis_index("row")
    col_at = lax.axis_index("col")
    planes, h_block, k_block = intensity.shape
    groups = col_count // row_count
    fine_width = k_block // col_count
    pencil_rows = groups * fine_width
    levels = jnp.arange(planes, dtype=jnp.int32)
    swapped_table = jnp.swapaxes(punch_radius, 1, 2)
    outgoing = jnp.transpose(
        intensity.reshape(planes, h_block, col_count, fine_width), (2, 3, 0, 1)
    )
    arrived = lax.all_to_all(
        lax.all_to_all(outgoing, "col", split_axis=0, concat_axis=0, tiled=True),
        "row",
        split_axis=0,
        concat_axis=3,
        tiled=True,
    )
    pencil_h = (
        h_block * row_at
        + k_block * jnp.arange(groups, dtype=jnp.int32)[:, None]
        + fine_width * col_at
        + jnp.arange(fine_width, dtype=jnp.int32)[None, :]
    ).reshape(-1)
    whole_k = jnp.arange(N, dtype=jnp.int32)
    mirrored = arrived.reshape(pencil_rows, planes, N)
    pencil_input = jnp.transpose(
        intensity.reshape(planes, groups, col_count, fine_width, k_block), (1, 2, 3, 0, 4)
    )
    direct = lax.all_to_all(pencil_input, "col", split_axis=1, concat_axis=4, tiled=True).reshape(
        pencil_rows, planes, N
    )
    keep_mask = keep_map(pencil_h, whole_k, punch_radius, levels)
    keep_swap = keep_map(pencil_h, whole_k, swapped_table, levels)
    counts = jnp.maximum(keep_mask + keep_swap, 1.0)
    symmetric = ((keep_mask * direct + keep_swap * mirrored) / counts).astype(jnp.bfloat16)
    row_total = pencil_rows * planes
    flat_rows = symmetric.reshape(row_total, N).astype(jnp.float32)
    part_re, part_im = spectral_lead(flat_rows)
    freq_width = N // (row_count * col_count)
    sectioned = jnp.stack([part_re, part_im]).reshape(
        2, row_count, col_count, freq_width, row_total
    )
    spectra = lax.all_to_all(
        lax.all_to_all(sectioned, "row", split_axis=1, concat_axis=1, tiled=True),
        "col",
        split_axis=2,
        concat_axis=2,
        tiled=True,
    )
    spectra = spectra.reshape(2, row_count, col_count, freq_width, groups, fine_width, planes)
    spectra = jnp.transpose(spectra, (0, 6, 3, 1, 4, 2, 5)).reshape(2, planes * freq_width, N)
    final_re, final_im = spectral(spectra[0], spectra[1])
    out_re = (final_re / N).reshape(planes, freq_width, N)
    out_im = (final_im / N).reshape(planes, freq_width, N)
    return (out_re, out_im)


RADIX = 4
HALVES = 2
CORES = 2
CURVE = 7
CODE_BITS = 102
UNIT = 2.0**-CODE_BITS
LIMIT = 60 * 1024 * 1024


def dot32(left, right):
    return jnp.dot(left, right, preferred_element_type=jnp.float32)


def butterfly(res, ims):
    even_re, odd_re = res[0] + res[2], res[0] - res[2]
    even_im, odd_im = ims[0] + ims[2], ims[0] - ims[2]
    pair_re, gap_re = res[1] + res[3], res[1] - res[3]
    pair_im, gap_im = ims[1] + ims[3], ims[1] - ims[3]
    out_re = (even_re + pair_re, odd_re - gap_im, even_re - pair_re, odd_re + gap_im)
    out_im = (even_im + pair_im, odd_im + gap_re, even_im - pair_im, odd_im - gap_re)
    return out_re, out_im


def encode(values):
    size = jnp.exp2(jnp.log2(jnp.abs(values)) * (1.0 / CURVE)) * 2.0 ** (CODE_BITS / CURVE)
    return jnp.where(values < 0, -jnp.round(size), jnp.round(size)).astype(jnp.int32).astype(jnp.int16)


def decode(codes):
    base = codes.astype(jnp.int32).astype(jnp.float32)
    square = base * base
    return (square * square) * (square * base)


def keep_scale(near, far, picked, distance):
    keep_mirror = distance >= dot32(near, picked)
    keep_direct = distance >= dot32(far, picked)
    scale = jnp.where(keep_mirror & keep_direct, 0.5 * UNIT, UNIT)
    return jnp.where(keep_mirror, scale, 0.0), jnp.where(keep_direct, scale, 0.0)


def build_tables(freq, time, flip, pick, size, lead_refs, minor_refs, half, layer_count, core):
    coarse_re, coarse_im, fine_re, fine_im = lead_refs
    fine = fine_re.shape[1]
    _, _, _, _, rows, width = freq.shape
    runs = rows // fine
    inner = runs // layer_count

    @pl.loop(0, RADIX * CORES * runs)
    def _(at):
        lead, rest = at // (CORES * runs), lax.rem(at, CORES * runs)
        side, run = rest // runs, lax.rem(rest, runs)
        owner = core + side * (1 - 2 * core)
        start = (half * layer_count + run // inner) * CORES * inner
        start = start + owner * inner + lax.rem(run, inner)
        big_re, big_im = coarse_re[start, lead], coarse_im[start, lead]
        low_re, low_im = fine_re[lead], fine_im[lead]
        place = pl.ds(pl.multiple_of(run * fine, fine), fine)
        for kind, full in (
            (0, big_re * low_re - big_im * low_im),
            (1, big_re * low_im + big_im * low_re),
        ):
            high = full.astype(jnp.bfloat16)
            freq[0, lead, side, kind, place] = high
            freq[1, lead, side, kind, place] = (full - high.astype(jnp.float32)).astype(
                jnp.bfloat16
            )

    base_re, base_im, step_re, step_im = minor_refs
    blocks = width // fine
    tile_runs = blocks // (CORES * RADIX)

    @pl.loop(0, RADIX * blocks)
    def _(at):
        lead, run = at // blocks, lax.rem(at, blocks)
        rel, rest = run // (blocks // CORES), lax.rem(run, blocks // CORES)
        owner = core + rel * (1 - 2 * core)
        start = (CORES * (rest // tile_runs) + owner) * tile_runs + lax.rem(rest, tile_runs)
        big_re, big_im = base_re[start], base_im[start]
        low_re, low_im = step_re[lead], step_im[lead]
        for kind, full in (
            (0, big_re * low_re - big_im * low_im),
            (1, big_re * low_im + big_im * low_re),
        ):
            high = full.astype(jnp.bfloat16)
            low = (full - high.astype(jnp.float32)).astype(jnp.bfloat16)
            for level, values in ((0, high), (1, low)):
                place = pl.ds(pl.multiple_of(level * width + run * fine, fine), fine)
                time[lead, place, kind * width : (kind + 1) * width] = values

    wide = flip.shape[0]
    piece = size // RADIX
    rows = lax.broadcasted_iota(jnp.int32, (wide, wide), 0)
    cols = lax.broadcasted_iota(jnp.int32, (wide, wide), 1)
    source = cols // piece % 2 * size + RADIX * (cols % piece) + cols // (2 * piece)
    flip[...] = (source == rows).astype(jnp.float32).astype(jnp.bfloat16)
    rows = lax.broadcasted_iota(jnp.int32, pick.shape, 0)
    cols = lax.broadcasted_iota(jnp.int32, pick.shape, 1)
    coord = (cols // size * CORES + core) * size + cols % size
    pick[...] = ((coord + SP // 2) // SP == rows).astype(jnp.float32).astype(jnp.bfloat16)


def plane_kernel(scale, value_ref, punch_ref, *refs):
    lead_refs, minor_refs, refs = refs[:4], refs[4:8], refs[8:]
    got_ref, raw, codes, tiles, mirror, sym, freq, time, part, other, stage = refs[:11]
    pick_ref, mask, flip_ref, mixed, bar_ref = refs[11:16]
    load_sem, in_send, in_recv, swap_sem, out_send, out_recv = refs[16:]
    row_count = lax.axis_size("row")
    col_count = lax.axis_size("col")
    row = lax.axis_index("row")
    col = lax.axis_index("col")
    core = lax.rem(col, CORES)
    deep, span = stage.shape[1], stage.shape[3]
    size = tiles.shape[-1]
    layer = lax.rem(col // CORES, deep)
    base = col - core - CORES * layer
    half_at = col // (CORES * deep)
    mine = row * deep + layer
    lot = row_count * deep
    me = row * col_count + col
    devices = row_count * col_count
    twin = {"col": col + 1 - 2 * core}

    def plane_of(at):
        step = lax.rem(at, lot)
        step = core * (lot - 1 - step) + (1 - core) * step
        high, low = row // 2 + step // deep // 2, lax.rem(row, 2) + lax.rem(step // deep, 2)
        to_row = lax.rem(high, row_count // 2) * 2 + lax.rem(low, 2)
        return at // lot * lot + to_row * deep + lax.rem(layer + step, deep)

    def load(at):
        slot = lax.rem(at, 2)
        return pltpu.make_async_copy(
            value_ref.at[plane_of(at)], raw.at[slot], load_sem.at[slot]
        )

    load(0).start()

    def device(place):
        return {"row": place // col_count, "col": lax.rem(place, col_count)}

    barrier = pltpu.get_barrier_semaphore()

    @pl.loop(1, devices)
    def _(step):
        pl.semaphore_signal(barrier, inc=1, device_id=device(lax.rem(me + step, devices)))

    pl.semaphore_wait(barrier, devices - 1)

    def swap(turn):
        return pltpu.make_async_remote_copy(
            src_ref=tiles.at[turn, :, :, 1 - core],
            dst_ref=mirror,
            send_sem=swap_sem.at[turn, 0],
            recv_sem=swap_sem.at[turn, 1],
            device_id=twin,
        )

    def trade(turn):
        return pltpu.make_async_remote_copy(
            src_ref=part.at[1],
            dst_ref=other,
            send_sem=swap_sem.at[turn, 2],
            recv_sem=swap_sem.at[turn, 3],
            device_id=twin,
        )

    def in_copy(turn, target, source):
        to_row = target // col_count
        to_col = lax.rem(target, col_count)
        from_row = source // col_count
        from_col = lax.rem(source, col_count)
        plane = turn * lot + to_row * deep + lax.rem(to_col // CORES, deep)
        return pltpu.make_async_remote_copy(
            src_ref=codes.at[plane, lax.rem(to_col, CORES)],
            dst_ref=tiles.at[turn, from_row, from_col // CORES, lax.rem(from_col, CORES)],
            send_sem=in_send.at[turn, target],
            recv_sem=in_recv.at[turn, source],
            device_id=device(target),
        )

    def inside(turn):
        return pltpu.make_async_copy(
            codes.at[turn * lot + mine, core],
            tiles.at[turn, row, col // CORES, core],
            load_sem.at[2 + turn],
        )

    def target_of(plane, half, side):
        spot = lax.rem(plane, lot)
        to_col = (half * deep + lax.rem(spot, deep)) * CORES + side
        return spot // deep * col_count + to_col

    @pl.loop(0, 2 * lot)
    def _(at):
        turn = at // lot

        @pl.when(at + 1 < 2 * lot)
        def _():
            load(at + 1).start()

        load(at).wait()
        plane = plane_of(at)
        codes[plane] = encode(raw[lax.rem(at, 2)]).reshape(codes.shape[1:])

        @pl.when(turn == 0)
        def _():
            for side in range(CORES):
                in_copy(0, target_of(plane, 1 - half_at, side), me).start()

        for side in range(CORES):
            target = target_of(plane, half_at, side)

            @pl.when(target != me)
            def _():
                in_copy(turn, target, me).start()

    for turn in range(2):
        inside(turn).start()

    build_tables(
        freq, time, flip_ref, pick_ref, size, lead_refs, minor_refs, half_at, deep, core
    )

    width = 2 * size
    piece = width // RADIX
    pairs = row_count // 2
    rows = lax.broadcasted_iota(jnp.int32, (size, width), 0)
    cols = lax.broadcasted_iota(jnp.int32, (size, width), 1)
    row_off = (rows + SP // 2) % SP - SP // 2
    col_off = (cols + SP // 2) % SP - SP // 2
    distance = (row_off * row_off + col_off * col_off).astype(jnp.float32)

    node_rows = lax.broadcasted_iota(jnp.int32, (size, bar_ref.shape[-1]), 0)
    node_cols = lax.broadcasted_iota(jnp.int32, (size, bar_ref.shape[-1]), 1)

    def build_masks(turn):
        @pl.loop(0, col_count)
        def _(tile):
            nodes = (node_rows + (tile * size + SP // 2)) // SP == node_cols
            nodes = nodes.astype(jnp.float32).astype(jnp.bfloat16)
            near = dot32(nodes, bar_ref[turn]).astype(jnp.bfloat16)
            far = lax.dot_general(
                nodes,
                bar_ref[turn],
                (((1,), (1,)), ((), ())),
                preferred_element_type=jnp.float32,
            ).astype(jnp.bfloat16)
            for pair in range(pairs):
                spot = pl.ds(pair * width, width)
                both = keep_scale(near, far, pick_ref[:, spot], distance)
                for kind in range(2):
                    mask[kind, tile, :, spot] = both[kind].astype(mask.dtype)

    bar_ref[...] = jnp.zeros_like(bar_ref)
    grid_nodes = punch_ref.shape[-1]
    for turn in range(2):
        level = turn * lot + mine
        node = (level + SP // 2) // SP
        off = level - SP * node
        limit = (punch_ref[node] - off * off).astype(jnp.float32).astype(jnp.bfloat16)
        bar_ref[turn, :grid_nodes, :grid_nodes] = limit

    build_masks(0)

    def take(turn):
        @pl.loop(1, devices)
        def _(step):
            in_copy(turn, me, lax.rem(me + step, devices)).wait_recv()

        inside(turn).wait()
        swap(turn).start()

    take(0)

    @pl.loop(0, lot)
    def _(at):
        plane = plane_of(lot + at)
        for side in range(CORES):
            in_copy(1, target_of(plane, 1 - half_at, side), me).start()

    def blend(turn, block, parity, reflected):
        tile = CORES * block + parity
        run = size // RADIX
        offset = pl.multiple_of(parity * run, run)
        for pair in range(pairs):
            spot = pl.ds(pair * width, width)
            turned = jnp.concatenate(
                [decode(tiles[turn, 2 * pair + up, block, parity]).T for up in range(2)], axis=1
            )
            across = jnp.concatenate(
                [decode(reflected(block, 2 * pair + up)) for up in range(2)], axis=1
            )
            by_mirror, by_direct = (
                mask[kind, tile, :, spot].astype(jnp.float32) for kind in range(2)
            )
            total = by_mirror * across + by_direct * turned
            lanes = mixed.shape[-1]
            strips = width // lanes
            for strip in range(strips):
                mixed[pair * strips + strip] = total[:, strip * lanes : (strip + 1) * lanes]
            for lead in range(RADIX):
                at = lead * row_count + block
                values = jnp.concatenate(
                    [
                        mixed[pair * strips + strip, pl.ds(lead, run, stride=RADIX), :]
                        for strip in range(strips)
                    ],
                    axis=1,
                )
                part[
                    at // (2 * RADIX), at // 2 % RADIX, at % 2, pl.ds(offset, run), spot
                ] = values.astype(part.dtype)

    def sort_columns():
        for lead in range(RADIX):
            start = lead * row_count // 2
            natural = part[start // RADIX, start % RADIX : start % RADIX + row_count // 2]
            natural = natural.reshape(-1, pairs * width)
            for pair in range(pairs):
                ready = dot32(natural[:, pair * width : (pair + 1) * width], flip_ref[...])
                ready = ready.astype(sym.dtype)
                for other_lead in range(RADIX):
                    spot = (other_lead * pairs + pair) * piece
                    sym[lead, :, spot : spot + piece] = ready[
                        :, other_lead * piece : (other_lead + 1) * piece
                    ]

    def blend_all(turn):
        @pl.loop(0, row_count)
        def _(block):
            blend(turn, block, core, lambda at, up: tiles[turn, at, up, core])

        swap(turn).wait()

        @pl.loop(0, row_count)
        def _(block):
            blend(turn, block, 1 - core, lambda at, up: mirror[at, up])

        sort_columns()

    count = part.shape[3]

    def first_all(turn):
        for side in (1, 0):
            res, ims = [], []
            for lead in range(RADIX):
                data = sym[lead]
                high = freq[0, lead, side].reshape(2 * count, -1)
                low = freq[1, lead, side].reshape(2 * count, -1)
                both = dot32(high, data) + dot32(low, data)
                res.append(both[:count])
                ims.append(both[count:])
            out_re, out_im = butterfly(res, ims)
            for block in range(RADIX):
                part[side, block, 0] = out_re[block].astype(part.dtype)
                part[side, block, 1] = out_im[block].astype(part.dtype)
            if side:
                trade(turn).start()

    def partner(step):
        high, low = row // 2 + step // 2, lax.rem(row, 2) + lax.rem(step, 2)
        return lax.rem(high, row_count // 2) * 2 + lax.rem(low, 2)

    def out_copy(turn, step, shift):
        to_row = partner(step)
        to_layer = lax.rem(layer + shift, deep)
        return pltpu.make_async_remote_copy(
            src_ref=stage.at[to_row, to_layer],
            dst_ref=got_ref.at[turn, mine],
            send_sem=out_send.at[turn, step * deep + shift],
            recv_sem=out_recv.at[turn, step * deep + shift],
            device_id={"row": to_row, "col": base + CORES * to_layer + core},
        )

    def own(turn):
        return pltpu.make_async_copy(
            stage.at[row, layer], got_ref.at[turn, mine], out_recv.at[turn, 0]
        )

    half = part.shape[-1] // RADIX

    def second_all(turn):
        @pl.loop(0, row_count)
        def _(tick):
            away = row_count - 1 - tick
            step = core * (lax.rem(tick, 2) * 2 + tick // 2)
            step = step + (1 - core) * (lax.rem(away, 2) * 2 + away // 2)
            block = partner(step)
            if turn:
                for shift in range(1, deep):
                    out_copy(0, step, shift).wait_send()

                @pl.when(step != 0)
                def _():
                    out_copy(0, step, 0).wait_send()

                @pl.when(step == 0)
                def _():
                    own(0).wait()

            res, ims = [], []
            for lead in range(RADIX):
                data = jnp.concatenate(
                    [
                        jnp.concatenate(
                            [
                                part[0, block, kind, :, lead * half : (lead + 1) * half],
                                other[block, kind, :, lead * half : (lead + 1) * half],
                            ],
                            axis=1,
                        )
                        for kind in range(2)
                    ],
                    axis=0,
                )
                broad = data.shape[1]
                both = dot32(data, time[lead, :broad]) + dot32(data, time[lead, broad:])
                res.append(both[:count, :broad] - both[count:, broad:])
                ims.append(both[:count, broad:] + both[count:, :broad])
            out_re, out_im = butterfly(res, ims)
            for kind, values in ((0, out_re), (1, out_im)):
                for quarter in range(RADIX):
                    ready = (values[quarter] * scale).astype(stage.dtype)
                    for at in range(deep):
                        stage[block, at, kind, :, quarter * broad : (quarter + 1) * broad] = (
                            ready[at * span : (at + 1) * span]
                        )
            for shift in range(1, deep):
                out_copy(turn, step, shift).start()

            @pl.when(step != 0)
            def _():
                out_copy(turn, step, 0).start()

            @pl.when(step == 0)
            def _():
                own(turn).start()

    blend_all(0)
    first_all(0)
    trade(0).wait()
    second_all(0)
    build_masks(1)
    take(1)
    blend_all(1)
    first_all(1)
    trade(1).wait()
    second_all(1)
    own(1).wait()
    for turn in range(2):
        for at in range(1, lot):
            out_copy(turn, at // deep, at % deep).wait_recv()
    for at in range(1, lot):
        out_copy(1, at // deep, at % deep).wait_send()

    for turn in range(2):

        @pl.loop(1, devices)
        def _(step):
            in_copy(turn, lax.rem(me + step, devices), me).wait_send()


def angles(first_ids, second_ids, period):
    turns = np.mod(np.multiply.outer(first_ids, second_ids), period) * (2.0 * np.pi / period)
    return np.cos(turns).astype(np.float32), np.sin(turns).astype(np.float32)


def work(intensity, punch_radius, scale, row_count, col_count):
    planes, h_block, size = intensity.shape
    devices = row_count * col_count
    deep = col_count // (HALVES * CORES)
    lot = row_count * deep
    length = row_count * h_block
    broad = length // RADIX
    width = row_count * size
    span = length // devices
    rows = deep * span
    bf16 = jnp.bfloat16
    fine = 16
    room = punch_radius.shape[-1]
    room += -room % 256
    lead_ids = np.arange(RADIX)
    fine_ids = np.arange(fine)
    samples = RADIX * np.arange(broad)[None, :] + lead_ids[:, None]
    minor = np.arange(broad)
    coarse = [part[:, :, None] for part in angles(fine * np.arange(broad // fine), samples, length)]
    low = [part.transpose(1, 0, 2) for part in angles(fine_ids, samples, length)]
    base = [
        part[:, None] for part in angles(RADIX * fine * np.arange(broad // fine), minor, length)
    ]
    step = angles(RADIX * fine_ids[None, :] + lead_ids[:, None], minor, length)
    small = [jnp.asarray(part) for part in [*coarse, *low, *base, *step]]
    tile_shape = (row_count, col_count // CORES, CORES, size, size)
    return pl.pallas_call(
        lambda *refs: plane_kernel(scale, *refs),
        out_shape=jax.ShapeDtypeStruct((2, lot, 2, span, length), bf16),
        in_specs=[pl.BlockSpec(memory_space=pl.ANY)]
        + [pl.BlockSpec(memory_space=pltpu.VMEM)] * (1 + len(small)),
        out_specs=pl.BlockSpec(memory_space=pl.ANY),
        scratch_shapes=[
            pltpu.VMEM((2, h_block, size), jnp.float32),
            pltpu.VMEM((planes, CORES, size, size), jnp.int16),
            pltpu.VMEM((2,) + tile_shape, jnp.int16),
            pltpu.VMEM((row_count, row_count, size, size), jnp.int16),
            pltpu.VMEM((RADIX, broad, width), bf16),
            pltpu.VMEM((2, RADIX, CORES, 2, rows, broad), bf16),
            pltpu.VMEM((RADIX, 2 * broad, 2 * broad), bf16),
            pltpu.VMEM((CORES, RADIX, 2, rows, width), bf16),
            pltpu.VMEM((RADIX, 2, rows, width), bf16),
            pltpu.VMEM((RADIX, deep, 2, span, length), bf16),
            pltpu.VMEM((room, width), bf16),
            pltpu.VMEM((2, col_count, size, width), bf16),
            pltpu.VMEM((2 * size, 2 * size), bf16),
            pltpu.VMEM((width // 128, size, 128), jnp.float32),
            pltpu.VMEM((2, room, room), bf16),
            pltpu.SemaphoreType.DMA((4,)),
            pltpu.SemaphoreType.DMA((2, devices)),
            pltpu.SemaphoreType.DMA((2, devices)),
            pltpu.SemaphoreType.DMA((2, 4)),
            pltpu.SemaphoreType.DMA((2, lot)),
            pltpu.SemaphoreType.DMA((2, lot)),
        ],
        compiler_params=pltpu.CompilerParams(
            collective_id=0, has_side_effects=True, vmem_limit_bytes=LIMIT
        ),
        cost_estimate=pl.CostEstimate(
            flops=140 * 10**9, bytes_accessed=10**7, transcendentals=0
        ),
    )(intensity, punch_radius, *small)


def widen_kernel(got_ref, re_ref, im_ref, narrow, wide, in_sem, out_sem):
    count, slots = got_ref.shape[0], narrow.shape[0]

    def load(at):
        return pltpu.make_async_copy(got_ref.at[at], narrow.at[at % slots], in_sem.at[at % slots])

    def stores(at):
        return [
            pltpu.make_async_copy(
                wide.at[at % slots, kind], ref.at[at], out_sem.at[at % slots, kind]
            )
            for kind, ref in ((0, re_ref), (1, im_ref))
        ]

    for at in range(min(slots, count)):
        load(at).start()
    for at in range(count):
        load(at).wait()
        if at >= slots:
            for store in stores(at - slots):
                store.wait()
        for kind in range(2):
            wide[at % slots, kind] = narrow[at % slots, kind].astype(jnp.float32)
        for store in stores(at):
            store.start()
        if at + slots < count:
            load(at + slots).start()
    for at in range(max(count - slots, 0), count):
        for store in stores(at):
            store.wait()


def widen(got):
    count, _, span, length = got.shape
    slots = 8
    shape = jax.ShapeDtypeStruct((count, span, length), jnp.float32)
    return pl.pallas_call(
        widen_kernel,
        out_shape=(shape, shape),
        in_specs=[pl.BlockSpec(memory_space=pl.ANY)],
        out_specs=(pl.BlockSpec(memory_space=pl.ANY),) * 2,
        scratch_shapes=[
            pltpu.VMEM((slots, 2, span, length), got.dtype),
            pltpu.VMEM((slots, 2, span, length), jnp.float32),
            pltpu.SemaphoreType.DMA((slots,)),
            pltpu.SemaphoreType.DMA((slots, 2)),
        ],
        compiler_params=pltpu.CompilerParams(vmem_limit_bytes=LIMIT),
    )(got)


def plane_body(intensity, punch_radius):
    row_count = lax.axis_size("row")
    col_count = lax.axis_size("col")
    planes, h_block, _ = intensity.shape
    got = work(intensity, punch_radius, 1.0 / (h_block * row_count), row_count, col_count)
    return tuple(widen(got.reshape((planes,) + got.shape[2:])))


def body(intensity, punch_radius):
    row_count = lax.axis_size("row")
    col_count = lax.axis_size("col")
    planes, _, k_block = intensity.shape
    by_plane = row_count == RADIX and col_count == HALVES * RADIX
    by_plane = by_plane and 2 * planes == row_count * col_count and k_block % 256 == 0
    return (plane_body if by_plane else pencil_body)(intensity, punch_radius)


def solution(mesh):
    in_specs = (P(None, "row", "col"), P())
    out_specs = (P(None, ("row", "col"), None), P(None, ("row", "col"), None))
    return jax.shard_map(body, mesh=mesh, in_specs=in_specs, out_specs=out_specs, check_vma=False)
```
